32 devices in a mesh: dp: 8 (over z, y), tensor: 4 (over x, core).
Axes of the slice: x: 2, y: 2, z: 4, core: 2. Of those that a mesh axis runs over, the one named last changes fastest.
Arguments:
- tokens: bfloat16 [4096, 1024], P('dp'), may hold values from -6 to 6
- cotangent: bfloat16 [4096, 1024], P('dp'), may hold values from -6 to 6
- segment: int32 [4096], P('dp'), may hold values from 0 to 31, never falling along the last dimension, each value on 1 to 384 neighbouring positions
- norm_gain: float32 [1024], replicated, may hold values from 0.5 to 1.5
- gate_weight: bfloat16 [1024, 2048], P(None, 'tensor'), may hold values from -0.1875 to 0.1875
- value_weight: bfloat16 [1024, 2048], P(None, 'tensor'), may hold values from -0.1875 to 0.1875
- step_weight: bfloat16 [1024, 32], P(None, 'tensor'), may hold values from -0.1875 to 0.1875
- state_weight: bfloat16 [1024, 256], replicated, may hold values from -0.1875 to 0.1875
- value_conv: float32 [4, 2048], P(None, 'tensor'), may hold values from -3 to 3
- value_conv_bias: float32 [2048], P('tensor'), may hold values from -3 to 3
- state_conv: float32 [4, 256], replicated, may hold values from -3 to 3
- state_conv_bias: float32 [256], replicated, may hold values from -3 to 3
- step_bias: float32 [32], P('tensor'), may hold values from -6 to -2
- decay_log: float32 [32], P('tensor'), may hold values from 0 to 2.77
- skip_gain: float32 [32], P('tensor'), may hold values from 0.5 to 1.5
- gated_gain: float32 [2048], P('tensor'), may hold values from 0.5 to 1.5
- out_weight: bfloat16 [2048, 1024], P('tensor'), may hold values from -0.125 to 0.125
Outputs:
- mixed: bfloat16 [4096, 1024], P(('dp', 'tensor'))
- grad_tokens: bfloat16 [4096, 1024], P(('dp', 'tensor'))
- grad_norm_gain: float32 [1024], replicated
- grad_gate_weight: float32 [1024, 2048], P('dp', 'tensor')
- grad_value_weight: float32 [1024, 2048], P('dp', 'tensor')
- grad_step_weight: float32 [1024, 32], P('dp', 'tensor')
- grad_state_weight: float32 [1024, 256], P('dp')
- grad_value_conv: float32 [4, 2048], P(None, 'tensor')
- grad_value_conv_bias: float32 [2048], P('tensor')
- grad_state_conv: float32 [4, 256], replicated
- grad_state_conv_bias: float32 [256], replicated
- grad_step_bias: float32 [32], P('tensor')
- grad_decay_log: float32 [32], P('tensor')
- grad_skip_gain: float32 [32], P('tensor')
- grad_gated_gain: float32 [2048], P('tensor')
- grad_out_weight: float32 [2048, 1024], P('tensor', 'dp')
The draws below stay inside these ranges and needn't reach their ends.
Inputs may be any that keep to these rules, and one draw needn't show every extreme that they name: Segment numbers never fall along the tokens; each segment covers 1 to 384 tokens, and one covers exactly that many.
All inputs are finite; a program needn't handle non-finite values.
Results may differ from the reference program's by a relative error of at most 0.0083.
Values sent between devices are 32-bit elements; how exact they have to be, the bound alone decides.
No kernel may reach another device: no remote copies, remote signals or barrier semaphores. Data moves between devices by JAX's collectives and lax.ppermute only.
A program may use at most 128 MiB of HBM per device.

```python
import math
from functools import partial
import jax
import jax.numpy as jnp
import numpy as np
from jax import lax

D = 1024
H = 32
N = 128
K = 4
STRETCH = 256
SEQ_LEN = 512
DI = 2048
TOKENS = 4096


def spiked(values, stream_key, source, target, parts, factor):
    def block_of(dim):
        return (jnp.arange(values.shape[dim]) // (values.shape[dim] // parts)).reshape((-1,) + (1,) * (values.ndim - 1 - dim))

    near = jax.random.permutation(stream_key, parts)[block_of(target)]
    other_side = (block_of(target) + parts // 2) % parts
    return jnp.where((block_of(source) == near) | (block_of(source) == other_side), factor * values, values)


def levels(stream_key, extent, cuts, least, top_value):
    factor_of, own = 1.0, jax.random.fold_in(stream_key, 6)
    for axis_at, parts in cuts:
        steps = jnp.exp(jax.random.uniform(jax.random.fold_in(own, axis_at), (parts,), jnp.float32, least / len(cuts), top_value / len(cuts)))
        factor_of = factor_of * jnp.repeat(steps, extent[axis_at] // parts).reshape([-1 if axis == axis_at else 1 for axis in range(len(extent))])
    return factor_of


def profile(count, total, bound, skew):
    weights = [(1 << 20) // math.isqrt(standing ** skew) + 1 for standing in range(2, count + 1)]
    rest, holding = total - bound - (count - 1), [1] * (count - 1)
    while rest > 0:
        candidates = [i for i in range(count - 1) if holding[i] < bound]
        mass, remaining = sum([weights[i] for i in candidates]), rest
        for i in candidates:
            addition = min(bound - holding[i], max(1, remaining * weights[i] // mass), rest)
            holding[i] = holding[i] + addition
            rest = rest - addition
    return np.array([bound] + holding)


def uneven(stream_key, amount, total, bound, skew):
    if amount == 2:
        one = jax.random.randint(stream_key, (), max(1, total - bound), min(bound, total - 1) + 1)
        return jnp.stack([one, total - one])
    sizes = jnp.asarray(profile(amount, total, bound, skew), jnp.int32)
    pairs = (amount - 1) // 2
    source_of, taker = sizes[1:1 + 2 * pairs:2], sizes[2:2 + 2 * pairs:2]
    margin = jnp.minimum(source_of - 1, bound - taker)
    moved = jax.random.randint(jax.random.fold_in(stream_key, 1), (pairs,), 0, 1 << 20) % (margin + 1)
    sizes = sizes.at[1:1 + 2 * pairs:2].set(source_of - moved).at[2:2 + 2 * pairs:2].set(taker + moved)
    return sizes[jax.random.permutation(jax.random.fold_in(stream_key, 2), amount)]


def normal_values(rng, dims, width, bound, split=(), kind=jnp.bfloat16):
    result = width * jax.random.normal(rng, dims, jnp.float32)
    if split:
        result = result * levels(rng, dims, split, -0.22, 0.18)
    return jnp.clip(result, -bound, bound).astype(kind)


def bell_draw_with(key, extent, spread, reach, shards, heavy, held_as=jnp.bfloat16):
    entries = spread * jax.random.normal(key, extent, jnp.float32)
    if shards:
        entries = entries * levels(key, extent, shards, -0.22, 0.18)
    return jnp.clip(spiked(entries, jax.random.fold_in(key, 3), *heavy), -reach, reach).astype(held_as)


def setup_inputs(seed: int = 0) -> dict:
    arg_keys = jax.random.split(jax.random.key(seed), 18)
    tokens = normal_values(arg_keys[0], (TOKENS, D), 1.0, 6.0, ((0, 8),))
    cotangent = bell_draw_with(arg_keys[1], (TOKENS, D), 1.0, 6.0, ((0, 8),), (0, 1, 8, 2.0))
    segment = jnp.searchsorted(jnp.cumsum(uneven(arg_keys[2], TOKENS // 128, TOKENS, 3 * SEQ_LEN // 4, 1)), jnp.arange(TOKENS), side="right").astype(jnp.int32)
    norm_gain = jnp.clip(1.0 + 0.1 * jax.random.normal(arg_keys[3], (D,), jnp.float32), 0.5, 1.5)
    gate_weight = normal_values(arg_keys[4], (D, DI), D ** -0.5, 0.1875, ((1, 4),))
    value_weight = normal_values(arg_keys[5], (D, DI), D ** -0.5, 0.1875, ((1, 4),))
    step_weight = normal_values(arg_keys[6], (D, H), D ** -0.5, 0.1875, ((1, 4),))
    state_weight = normal_values(arg_keys[7], (D, 2 * N), D ** -0.5, 0.1875)
    value_conv = normal_values(arg_keys[8], (K, DI), K ** -0.5, 3.0, ((1, 4),), jnp.float32)
    value_conv_bias = normal_values(arg_keys[9], (DI,), 0.5, 3.0, ((0, 4),), jnp.float32)
    state_conv = normal_values(arg_keys[10], (K, 2 * N), K ** -0.5, 3.0, (), jnp.float32)
    state_conv_bias = normal_values(arg_keys[11], (2 * N,), 0.5, 3.0, (), jnp.float32)
    step_bias = jnp.clip(-6.0 + 4.0 * jax.random.uniform(arg_keys[12], (H,), jnp.float32) ** levels(arg_keys[12], (H,), ((0, 4),), -0.2, 0.2), -6.0, -2.0)
    decay_log = jnp.clip(2.77 * jax.random.uniform(arg_keys[13], (H,), jnp.float32) ** levels(arg_keys[13], (H,), ((0, 4),), -0.2, 0.2), 0.0, 2.77)
    skip_gain = jnp.clip(0.5 + 1.0 * jax.random.uniform(arg_keys[14], (H,), jnp.float32) ** levels(arg_keys[14], (H,), ((0, 4),), -0.2, 0.2), 0.5, 1.5)
    gated_gain = jnp.clip(1.0 + 0.1 * jax.random.normal(arg_keys[15], (DI,), jnp.float32), 0.5, 1.5)
    out_weight = normal_values(arg_keys[16], (DI, D), DI ** -0.5, 0.125, ((0, 4),))
    return {"tokens": tokens, "cotangent": cotangent, "segment": segment, "norm_gain": norm_gain, "gate_weight": gate_weight, "value_weight": value_weight, "step_weight": step_weight, "state_weight": state_weight, "value_conv": value_conv, "value_conv_bias": value_conv_bias, "state_conv": state_conv, "state_conv_bias": state_conv_bias, "step_bias": step_bias, "decay_log": decay_log, "skip_gain": skip_gain, "gated_gain": gated_gain, "out_weight": out_weight}


epsilon = 1e-05
highest = lax.Precision.HIGHEST

def causal_conv(segment, inputs, weights, biases):
    kernel_width = weights.shape[0]
    length = inputs.shape[1]
    summed = jnp.zeros_like(inputs) + biases
    for tap_number in range(kernel_width):
        delay_steps = kernel_width - 1 - tap_number
        shifted = jnp.pad(inputs, ((0, 0), (delay_steps, 0), (0, 0)))[:, :length]
        prior_seg = jnp.pad(segment, ((0, 0), (delay_steps, 0)), constant_values=-1)[:, :length]
        keep_mask = jnp.where(prior_seg == segment, 1.0, 0.0).astype(inputs.dtype)
        summed = summed + weights[tap_number] * shifted * keep_mask[..., None]
    return summed

def conv_silu(segment, inputs, weights, biases):
    return jax.nn.silu(causal_conv(segment, inputs, weights, biases))

def mixer(segment, heads_here, conv_values, conv_states, step_raw, gate_z, step_bias, decay_log, skip_gain):
    seq_count, length, inner_width = conv_values.shape
    state_size = conv_states.shape[-1] // 2
    head_size = inner_width // heads_here
    stretch_count = length // STRETCH
    values = conv_values.reshape(seq_count, stretch_count, STRETCH, heads_here, head_size)
    keys_in = conv_states[..., :state_size].reshape(seq_count, stretch_count, STRETCH, state_size)
    queries = conv_states[..., state_size:].reshape(seq_count, stretch_count, STRETCH, state_size)
    steps_dt = jax.nn.softplus(step_raw + step_bias).reshape(seq_count, stretch_count, STRETCH, heads_here)
    decay_rates = -jnp.exp(decay_log)
    decay_sum = jnp.cumsum(steps_dt * decay_rates, axis=2)
    decay_heads = jnp.swapaxes(decay_sum, 2, 3)
    step_heads = jnp.swapaxes(steps_dt, 2, 3)
    stretch_segs = segment.reshape(seq_count, stretch_count, STRETCH)
    position = jnp.arange(STRETCH)
    causal = position[:, None] >= position[None, :]
    same_doc = (stretch_segs[..., :, None] == stretch_segs[..., None, :]) & causal
    scores = jnp.einsum('bcqn,bckn->bcqk', queries, keys_in, precision=highest)
    decay_gap = jnp.minimum(decay_heads[..., :, None] - decay_heads[..., None, :], 0.0)
    weight = jnp.where(same_doc[:, :, None], jnp.exp(decay_gap), 0.0) * scores[:, :, None] * step_heads[:, :, :, None, :]
    local_out = jnp.einsum('bchqk,bckhp->bcqhp', weight, values, precision=highest)
    tail_live = stretch_segs == stretch_segs[..., -1:]
    tail_weight = jnp.where(tail_live[:, :, None, :], jnp.exp(decay_heads[..., -1:] - decay_heads), 0.0) * step_heads
    stretch_state = jnp.einsum('bchk,bckn,bckhp->bchnp', tail_weight, keys_in, values, precision=highest)
    carried = stretch_state[:, 0]
    pieces = [jnp.zeros_like(local_out[:, 0])]
    for stretch_index in range(1, stretch_count):
        boundary = stretch_segs[:, stretch_index - 1, -1:]
        live_rows = stretch_segs[:, stretch_index] == boundary
        factor = jnp.where(live_rows[..., None], jnp.exp(decay_sum[:, stretch_index]), 0.0)
        pieces.append(jnp.einsum('bqn,bhnp->bqhp', queries[:, stretch_index], carried, precision=highest) * factor[..., None])
        kept_state = stretch_segs[:, stretch_index, -1] == boundary[:, 0]
        carry_scale = jnp.where(kept_state[:, None], jnp.exp(decay_sum[:, stretch_index, -1]), 0.0)
        carried = stretch_state[:, stretch_index] + carry_scale[:, :, None, None] * carried
    across = jnp.stack(pieces, axis=1)
    output = local_out + across + skip_gain[:, None] * values
    return output.reshape(seq_count, length, inner_width) * jax.nn.silu(gate_z)

def forward_backward(params, tokens, cotangent, segment):
    norm_gain, gate_weight, value_weight, step_weight, state_weight, value_conv, value_conv_bias, state_conv, state_conv_bias, step_bias, decay_log, skip_gain, gated_gain, out_weight = params
    seq_count = segment.shape[0]
    model_width = tokens.shape[1]
    heads_here = step_weight.shape[1]
    inner_width = gate_weight.shape[1]

    def shaped(array):
        return array.reshape(seq_count, SEQ_LEN, array.shape[-1])
    inputs = tokens.astype(jnp.float32)
    inv_rms = lax.rsqrt(lax.optimization_barrier(jnp.mean(inputs * inputs, axis=-1, keepdims=True)) + epsilon)
    normed = (inputs * inv_rms * norm_gain).astype(jnp.bfloat16)
    gate_z = jnp.dot(normed, gate_weight, preferred_element_type=jnp.float32)
    value_raw = jnp.dot(normed, value_weight, preferred_element_type=jnp.float32)
    step_raw = jnp.dot(normed, step_weight, preferred_element_type=jnp.float32)
    state_raw = jnp.dot(normed, state_weight, preferred_element_type=jnp.float32)
    conv_values, value_back = jax.vjp(partial(conv_silu, segment), shaped(value_raw), value_conv, value_conv_bias)
    conv_states, state_back = jax.vjp(partial(conv_silu, segment), shaped(state_raw), state_conv, state_conv_bias)
    mixer_out, mixer_back = jax.vjp(partial(mixer, segment, heads_here), conv_values, conv_states, shaped(step_raw), shaped(gate_z), step_bias, decay_log, skip_gain)
    gated_in = mixer_out.reshape(-1, inner_width)
    inv_gate = lax.rsqrt(lax.optimization_barrier(jnp.mean(gated_in * gated_in, axis=-1, keepdims=True)) + epsilon)
    gated = (gated_in * inv_gate * gated_gain).astype(jnp.bfloat16)
    branch = jnp.dot(gated, out_weight, preferred_element_type=jnp.float32)
    mixed = (inputs + branch).astype(jnp.bfloat16)
    grad_gated = jnp.dot(cotangent, out_weight.T, preferred_element_type=jnp.float32)
    grad_out_weight = jnp.dot(gated.T, cotangent, preferred_element_type=jnp.float32)
    grad_gated_gain = lax.optimization_barrier(jnp.sum(grad_gated * gated_in * inv_gate, axis=0))
    dot_sums = lax.optimization_barrier(jnp.sum(grad_gated * gated_gain * gated_in, axis=-1, keepdims=True))
    grad_mixer = grad_gated * gated_gain * inv_gate - gated_in * (inv_gate * inv_gate * inv_gate) * dot_sums / inner_width
    grad_values, grad_states, grad_step_raw, grad_gate_z, grad_step_bias, grad_decay_log, grad_skip_gain = mixer_back(shaped(grad_mixer))
    grad_value_raw, grad_value_conv, grad_value_conv_bias = value_back(grad_values)
    grad_state_raw, grad_state_conv, grad_state_conv_bias = state_back(grad_states)
    gate_low = grad_gate_z.reshape(-1, inner_width).astype(jnp.bfloat16)
    value_low = grad_value_raw.reshape(-1, inner_width).astype(jnp.bfloat16)
    step_low = grad_step_raw.reshape(-1, heads_here).astype(jnp.bfloat16)
    state_low = grad_state_raw.reshape(-1, state_weight.shape[1]).astype(jnp.bfloat16)
    grad_normed = jnp.dot(gate_low, gate_weight.T, preferred_element_type=jnp.float32) + jnp.dot(value_low, value_weight.T, preferred_element_type=jnp.float32) + jnp.dot(step_low, step_weight.T, preferred_element_type=jnp.float32) + jnp.dot(state_low, state_weight.T, preferred_element_type=jnp.float32)
    grad_gate_weight = jnp.dot(normed.T, gate_low, preferred_element_type=jnp.float32)
    grad_value_weight = jnp.dot(normed.T, value_low, preferred_element_type=jnp.float32)
    grad_step_weight = jnp.dot(normed.T, step_low, preferred_element_type=jnp.float32)
    grad_state_weight = jnp.dot(normed.T, state_low, preferred_element_type=jnp.float32)
    grad_norm_gain = lax.optimization_barrier(jnp.sum(grad_normed * inputs * inv_rms, axis=0))
    norm_sums = lax.optimization_barrier(jnp.sum(grad_normed * norm_gain * inputs, axis=-1, keepdims=True))
    grad_tokens = (grad_normed * norm_gain * inv_rms - inputs * (inv_rms * inv_rms * inv_rms) * norm_sums / model_width + cotangent.astype(jnp.float32)).astype(jnp.bfloat16)
    grads = (grad_norm_gain, grad_gate_weight, grad_value_weight, grad_step_weight, grad_state_weight, grad_value_conv, grad_value_conv_bias, grad_state_conv, grad_state_conv_bias, grad_step_bias, grad_decay_log, grad_skip_gain, grad_gated_gain, grad_out_weight)
    return ((mixed, grad_tokens), grads)

def reference(tokens, cotangent, segment, norm_gain, gate_weight, value_weight, step_weight, state_weight, value_conv, value_conv_bias, state_conv, state_conv_bias, step_bias, decay_log, skip_gain, gated_gain, out_weight):
    params = (norm_gain, gate_weight, value_weight, step_weight, state_weight, value_conv, value_conv_bias, state_conv, state_conv_bias, step_bias, decay_log, skip_gain, gated_gain, out_weight)
    total_seqs = segment.shape[0] // SEQ_LEN
    group_size = math.gcd(8, total_seqs)
    block_count = total_seqs // group_size
    model_width = tokens.shape[1]
    token_blocks = tokens.reshape(block_count, group_size * SEQ_LEN, model_width)
    cot_blocks = cotangent.reshape(block_count, group_size * SEQ_LEN, model_width)
    seg_blocks = segment.reshape(block_count, group_size, SEQ_LEN)

    def one_block(carry, pieces):
        outputs, grads = forward_backward(params, pieces[0], pieces[1], pieces[2])
        return (jax.tree.map(lambda left, right: left + right, carry, grads), outputs)
    initial = tuple((jnp.zeros(param.shape, jnp.float32) for param in params))
    totals, outputs = lax.scan(one_block, initial, (token_blocks, cot_blocks, seg_blocks))
    mixed = outputs[0].reshape(-1, model_width)
    grad_tokens = outputs[1].reshape(-1, model_width)
    return (mixed, grad_tokens, totals[0], totals[1], totals[2], totals[3], totals[4], totals[5], totals[6], totals[7], totals[8], totals[9], totals[10], totals[11], totals[12], totals[13])
```

```python
from functools import partial

import jax
import jax.numpy as jnp
from jax import lax
from jax.sharding import PartitionSpec as P

STRETCH = 256
SEQ_LEN = 512


epsilon = 1e-05
highest = lax.Precision.HIGHEST


def swap(array, axis, bit):
    size = lax.axis_size(axis)
    return lax.ppermute(array, axis, [(i, i ^ bit) for i in range(size)])


def bits_of(size):
    assert size & (size - 1) == 0
    return [1 << i for i in range(size.bit_length() - 1)]


def slot_order(bits):
    order = [0]
    for bit in reversed(bits):
        order = order + [slot | bit for slot in order]
    return order


def halving(keep, send, axis, bits):
    for step, bit in enumerate(bits):
        got = swap(send, axis, bit)
        half = keep.shape[0] // 2
        if step + 1 < len(bits):
            send = keep[half:] + got[half:]
            keep = keep[:half] + got[:half]
        else:
            keep = keep + got
    return keep[0]


def scatter_sum(pieces, axis, bits):
    me = lax.axis_index(axis)
    slots = [lax.dynamic_index_in_dim(pieces, me ^ slot, 0) for slot in slot_order(bits)]
    half = len(slots) // 2
    return halving(jnp.concatenate(slots[:half]), jnp.concatenate(slots[half:]), axis, bits)


def all_sum(array, axis):
    for bit in bits_of(lax.axis_size(axis)):
        array = array + swap(array, axis, bit)
    return array


def causal_conv(segment, inputs, weights, biases):
    kernel_width = weights.shape[0]
    length = inputs.shape[1]
    summed = jnp.zeros_like(inputs) + biases
    for tap_number in range(kernel_width):
        delay_steps = kernel_width - 1 - tap_number
        shifted = jnp.pad(inputs, ((0, 0), (delay_steps, 0), (0, 0)))[:, :length]
        prior_seg = jnp.pad(segment, ((0, 0), (delay_steps, 0)), constant_values=-1)[:, :length]
        keep_mask = jnp.where(prior_seg == segment, 1.0, 0.0).astype(inputs.dtype)
        summed = summed + weights[tap_number] * shifted * keep_mask[..., None]
    return summed


def conv_silu(segment, inputs, weights, biases):
    return jax.nn.silu(causal_conv(segment, inputs, weights, biases))


def mixer(
    segment, heads_here, conv_values, conv_states, step_raw, gate_z, step_bias, decay_log, skip_gain
):
    seq_count, length, inner_width = conv_values.shape
    state_size = conv_states.shape[-1] // 2
    head_size = inner_width // heads_here
    stretch_count = length // STRETCH
    values = conv_values.reshape(seq_count, stretch_count, STRETCH, heads_here, head_size)
    keys_in = conv_states[..., :state_size].reshape(seq_count, stretch_count, STRETCH, state_size)
    queries = conv_states[..., state_size:].reshape(seq_count, stretch_count, STRETCH, state_size)
    steps_dt = jax.nn.softplus(step_raw + step_bias).reshape(
        seq_count, stretch_count, STRETCH, heads_here
    )
    decay_rates = -jnp.exp(decay_log)
    decay_sum = jnp.cumsum(steps_dt * decay_rates, axis=2)
    decay_heads = jnp.swapaxes(decay_sum, 2, 3)
    step_heads = jnp.swapaxes(steps_dt, 2, 3)
    stretch_segs = segment.reshape(seq_count, stretch_count, STRETCH)
    position = jnp.arange(STRETCH)
    causal = position[:, None] >= position[None, :]
    same_doc = (stretch_segs[..., :, None] == stretch_segs[..., None, :]) & causal
    scores = jnp.einsum("bcqn,bckn->bcqk", queries, keys_in, precision=highest)
    decay_gap = jnp.minimum(decay_heads[..., :, None] - decay_heads[..., None, :], 0.0)
    weight = (
        jnp.where(same_doc[:, :, None], jnp.exp(decay_gap), 0.0)
        * scores[:, :, None]
        * step_heads[:, :, :, None, :]
    )
    local_out = jnp.einsum("bchqk,bckhp->bcqhp", weight, values, precision=highest)
    tail_live = stretch_segs == stretch_segs[..., -1:]
    tail_weight = (
        jnp.where(tail_live[:, :, None, :], jnp.exp(decay_heads[..., -1:] - decay_heads), 0.0)
        * step_heads
    )
    stretch_state = jnp.einsum(
        "bchk,bckn,bckhp->bchnp", tail_weight, keys_in, values, precision=highest
    )
    carried = stretch_state[:, 0]
    pieces = [jnp.zeros_like(local_out[:, 0])]
    boundary = stretch_segs[:, 0, -1:]
    live_rows = stretch_segs[:, 1] == boundary
    factor = jnp.where(live_rows[..., None], jnp.exp(decay_sum[:, 1]), 0.0)
    pieces.append(
        jnp.einsum("bqn,bhnp->bqhp", queries[:, 1], carried, precision=highest) * factor[..., None]
    )
    across = jnp.stack(pieces, axis=1)
    output = local_out + across + skip_gain[:, None] * values
    return output.reshape(seq_count, length, inner_width) * jax.nn.silu(gate_z)


def body(
    tokens,
    cotangent,
    segment,
    norm_gain,
    gate_weight,
    value_weight,
    step_weight,
    state_weight,
    value_conv,
    value_conv_bias,
    state_conv,
    state_conv_bias,
    step_bias,
    decay_log,
    skip_gain,
    gated_gain,
    out_weight,
):
    row_count, model_width = tokens.shape
    seq_count = row_count // SEQ_LEN
    tensor_parts = lax.axis_size("tensor")
    dp_parts = lax.axis_size("dp")
    rank = lax.axis_index("tensor")
    share = row_count // tensor_parts
    first_row = rank * share
    heads_here = step_weight.shape[1]
    inner_here = gate_weight.shape[1]
    inner_total = inner_here * tensor_parts
    state_width = state_weight.shape[1]
    own_states = state_width // tensor_parts
    seq_segments = segment.reshape(seq_count, SEQ_LEN)
    tensor_bits = bits_of(tensor_parts)
    dp_bits = bits_of(dp_parts)
    kernel_width = value_conv.shape[0]

    def shaped(array):
        return array.reshape(seq_count, SEQ_LEN, array.shape[-1])

    def own_rows(array):
        return lax.dynamic_slice_in_dim(array, first_row, share, 0)

    def own_columns(array):
        return lax.dynamic_slice_in_dim(array, rank * own_states, own_states, array.ndim - 1)

    def by_rows(array, parts):
        return array.reshape(parts, array.shape[0] // parts, array.shape[1])

    def by_columns(array, parts):
        return jnp.swapaxes(
            array.reshape(array.shape[0], parts, array.shape[1] // parts), 0, 1
        )

    inputs = tokens.astype(jnp.float32)
    inv_rms = lax.rsqrt(jnp.mean(inputs * inputs, axis=-1, keepdims=True) + epsilon)
    normed = (inputs * inv_rms * norm_gain).astype(jnp.bfloat16)
    gate_z = jnp.dot(normed, gate_weight, preferred_element_type=jnp.float32)
    value_raw = jnp.dot(normed, value_weight, preferred_element_type=jnp.float32)
    step_raw = jnp.dot(normed, step_weight, preferred_element_type=jnp.float32)
    state_raw = jnp.dot(normed, state_weight, preferred_element_type=jnp.float32)
    conv_values, value_back = jax.vjp(
        partial(conv_silu, seq_segments), shaped(value_raw), value_conv, value_conv_bias
    )
    conv_states = conv_silu(seq_segments, shaped(state_raw), state_conv, state_conv_bias)
    _, state_back = jax.vjp(
        partial(conv_silu, seq_segments),
        shaped(own_columns(state_raw)),
        own_columns(state_conv),
        own_columns(state_conv_bias),
    )
    mixer_out, mixer_back = jax.vjp(
        partial(mixer, seq_segments, heads_here),
        conv_values,
        conv_states,
        shaped(step_raw),
        shaped(gate_z),
        step_bias,
        decay_log,
        skip_gain,
    )
    gated_in = mixer_out.reshape(-1, inner_here)
    grad_gated = jnp.dot(cotangent, out_weight.T, preferred_element_type=jnp.float32)
    row_sums = all_sum(
        jnp.stack(
            [
                jnp.sum(gated_in * gated_in, axis=-1),
                jnp.sum(grad_gated * gated_gain * gated_in, axis=-1),
            ]
        ),
        "tensor",
    )
    inv_gate = lax.rsqrt(row_sums[0][:, None] / inner_total + epsilon)
    dot_sums = row_sums[1][:, None]
    gated = (gated_in * inv_gate * gated_gain).astype(jnp.bfloat16)
    grad_out_weight = jnp.dot(gated.T, cotangent, preferred_element_type=jnp.float32)
    grad_out_shard = scatter_sum(by_columns(grad_out_weight, dp_parts), "dp", dp_bits)
    branch = scatter_sum(
        by_rows(jnp.dot(gated, out_weight, preferred_element_type=jnp.float32), tensor_parts),
        "tensor",
        tensor_bits,
    )
    own_inputs = own_rows(inputs)
    mixed = (own_inputs + branch).astype(jnp.bfloat16)
    grad_gated_gain = jnp.sum(grad_gated * gated_in * inv_gate, axis=0)
    grad_mixer = (
        grad_gated * gated_gain * inv_gate
        - gated_in * (inv_gate * inv_gate * inv_gate) * dot_sums / inner_total
    )
    (
        grad_values,
        grad_states,
        grad_step_raw,
        grad_gate_z,
        grad_step_bias,
        grad_decay_log,
        grad_skip_gain,
    ) = mixer_back(shaped(grad_mixer))
    gate_low = grad_gate_z.reshape(-1, inner_here).astype(jnp.bfloat16)
    grad_gate_weight = jnp.dot(normed.T, gate_low, preferred_element_type=jnp.float32)
    gate_shard = scatter_sum(by_rows(grad_gate_weight, dp_parts), "dp", dp_bits)
    grad_states_own = scatter_sum(
        by_rows(grad_states.reshape(-1, state_width).T, tensor_parts), "tensor", tensor_bits
    ).T
    grad_value_raw, grad_value_conv, grad_value_conv_bias = value_back(grad_values)
    grad_state_raw, grad_state_conv, grad_state_conv_bias = state_back(shaped(grad_states_own))
    value_low = grad_value_raw.reshape(-1, inner_here).astype(jnp.bfloat16)
    step_low = grad_step_raw.reshape(-1, heads_here).astype(jnp.bfloat16)
    state_low = grad_state_raw.reshape(-1, own_states).astype(jnp.bfloat16)
    grad_value_weight = jnp.dot(normed.T, value_low, preferred_element_type=jnp.float32)
    value_shard = scatter_sum(by_rows(grad_value_weight, dp_parts), "dp", dp_bits)
    grad_state_weight = jnp.dot(state_low.T, normed, preferred_element_type=jnp.float32)
    grad_step_weight = jnp.dot(step_low.T, normed, preferred_element_type=jnp.float32)
    narrow = scatter_sum(
        by_columns(jnp.concatenate([grad_state_weight, grad_step_weight]), dp_parts), "dp", dp_bits
    )
    grad_normed_part = (
        jnp.dot(gate_low, gate_weight.T, preferred_element_type=jnp.float32)
        + jnp.dot(value_low, value_weight.T, preferred_element_type=jnp.float32)
        + jnp.dot(step_low, step_weight.T, preferred_element_type=jnp.float32)
        + jnp.dot(state_low, own_columns(state_weight).T, preferred_element_type=jnp.float32)
    )
    grad_norm_part = jnp.sum(grad_normed_part * inputs * inv_rms, axis=0)
    grad_normed = scatter_sum(by_rows(grad_normed_part, tensor_parts), "tensor", tensor_bits)
    own_inv = own_rows(inv_rms)
    norm_sums = jnp.sum(grad_normed * norm_gain * own_inputs, axis=-1, keepdims=True)
    grad_tokens = (
        grad_normed * norm_gain * own_inv
        - own_inputs * (own_inv * own_inv * own_inv) * norm_sums / model_width
        + own_rows(cotangent).astype(jnp.float32)
    ).astype(jnp.bfloat16)

    local = [
        grad_norm_part,
        grad_state_conv.reshape(-1),
        grad_state_conv_bias,
        grad_value_conv.reshape(-1),
        grad_value_conv_bias,
        grad_step_bias,
        grad_decay_log,
        grad_skip_gain,
        grad_gated_gain,
    ]
    packed = all_sum(jnp.concatenate(local), "dp")
    sums, start = [], 0
    for piece in local:
        sums.append(packed[start : start + piece.size])
        start += piece.size
    states_here = jnp.concatenate(
        [sums[1].reshape(kernel_width, own_states), sums[2][None], narrow[:own_states].T]
    )
    spread = jnp.concatenate(
        [jnp.where(rank == part, states_here, 0.0) for part in range(tensor_parts)], axis=1
    )
    shared = all_sum(jnp.concatenate([sums[0], spread.reshape(-1)]), "tensor")
    grad_norm_gain = shared[:model_width]
    spread = shared[model_width:].reshape(-1, state_width)
    return (
        mixed,
        grad_tokens,
        grad_norm_gain,
        gate_shard,
        value_shard,
        narrow[own_states:].T,
        spread[kernel_width + 1 :],
        sums[3].reshape(value_conv.shape),
        sums[4],
        spread[:kernel_width],
        spread[kernel_width],
        sums[5],
        sums[6],
        sums[7],
        sums[8],
        grad_out_shard,
    )


def solution(mesh):
    return jax.shard_map(
        body,
        mesh=mesh,
        in_specs=(
            P("dp", None),
            P("dp", None),
            P("dp"),
            P(),
            P(None, "tensor"),
            P(None, "tensor"),
            P(None, "tensor"),
            P(),
            P(None, "tensor"),
            P("tensor"),
            P(),
            P(),
            P("tensor"),
            P("tensor"),
            P("tensor"),
            P("tensor"),
            P("tensor", None),
        ),
        out_specs=(
            P(("dp", "tensor"), None),
            P(("dp", "tensor"), None),
            P(),
            P("dp", "tensor"),
            P("dp", "tensor"),
            P("dp", "tensor"),
            P("dp", None),
            P(None, "tensor"),
            P("tensor"),
            P(),
            P(),
            P("tensor"),
            P("tensor"),
            P("tensor"),
            P("tensor"),
            P("tensor", "dp"),
        ),
        check_vma=False,
    )
```

```python
from functools import partial

import jax
import jax.numpy as jnp
from jax import lax
from jax.experimental import pallas as pl
from jax.experimental.pallas import tpu as pltpu
from jax.sharding import PartitionSpec as P

STRETCH = 256
SEQ_LEN = 512


epsilon = 1e-05
highest = lax.Precision.HIGHEST
f32, bf16 = jnp.float32, jnp.bfloat16
LANES = 128
VMEM_LIMIT = 20 * 2**20


def swap(array, axis, bit):
    size = lax.axis_size(axis)
    return lax.ppermute(array, axis, [(i, i ^ bit) for i in range(size)])


def bits_of(size):
    assert size & (size - 1) == 0
    return [1 << i for i in range(size.bit_length() - 1)]


def slot_order(bits):
    order = [0]
    for bit in reversed(bits):
        order = order + [slot | bit for slot in order]
    return order


def halving_parts(keep, send, axis, bits, scope):
    terms, size = [keep], keep.shape[0]
    for step, bit in enumerate(bits):
        with jax.named_scope(f"{scope}{step}"):
            terms.append(swap(send, axis, bit))
        half = size // 2
        if half:
            send = sum(term[half:size] for term in terms[1:]) + keep[half:size]
        size = half
    return terms


def halving(keep, send, axis, bits, scope="plain"):
    first, *rest = [term[0] for term in halving_parts(keep, send, axis, bits, scope)]
    return first + sum(rest)


def scatter_sum(pieces, axis, bits):
    me = lax.axis_index(axis)
    slots = [lax.dynamic_index_in_dim(pieces, me ^ slot, 0) for slot in slot_order(bits)]
    half = len(slots) // 2
    return halving(jnp.concatenate(slots[:half]), jnp.concatenate(slots[half:]), axis, bits)


def all_sum(array, axis):
    for bit in bits_of(lax.axis_size(axis)):
        array = array + swap(array, axis, bit)
    return array


def dot(left, right, form="nn"):
    dims = {"nn": ((1,), (0,)), "nt": ((1,), (1,)), "tn": ((0,), (0,))}[form]
    return lax.dot_general(left, right, (dims, ((), ())), preferred_element_type=f32)


def dot_exact(left, right, form="nn"):
    high = left.astype(bf16)
    low = (left - high.astype(f32)).astype(bf16)
    return dot(high, right, form) + dot(low, right, form)


def sigmoid(v):
    return 1.0 / (1.0 + jnp.exp(-v))


def softplus(v):
    return jnp.maximum(v, 0.0) + jnp.log1p(jnp.exp(-jnp.abs(v)))


def iota(shape, dim):
    return lax.broadcasted_iota(jnp.int32, shape, dim)


def head_map(width, head_size):
    shape = (LANES, width)
    return jnp.where(iota(shape, 0) == iota(shape, 1) // head_size, 1.0, 0.0).astype(bf16)


def seg_columns(seg_ref):
    row = seg_ref[...].astype(f32)
    return jnp.transpose(jnp.broadcast_to(row, (LANES, row.shape[1])))


def delay_masks(columns, kernel_width):
    at = iota(columns.shape, 0)
    return {
        delay: jnp.where((pltpu.roll(columns, delay, 0) == columns) & (at >= delay), 1.0, 0.0)
        for delay in range(1, kernel_width)
    }


def column_of(values, lane):
    return values[:, lane : lane + 1]


def scan_matrix(size, upper):
    shape = (size, size)
    row, column = iota(shape, 0), iota(shape, 1)
    return jnp.where(column >= row if upper else column <= row, 1.0, 0.0)


def conv_chunk(raw, masks, taps, bias):
    kernel_width = taps.shape[0]
    summed = bias + taps[kernel_width - 1 :] * raw
    for delay, mask in masks.items():
        tap = kernel_width - 1 - delay
        summed = summed + taps[tap : tap + 1] * (pltpu.roll(raw, delay, 0) * mask)
    return summed


def head_rows(ref, scratch, row):
    scratch[row : row + 1, : ref.shape[1]] = ref[...]


def norm_kernel(tokens, norm_gain, normed, normed_t):
    for start in range(0, tokens.shape[0], LANES):
        rows = slice(start, start + LANES)
        values = tokens[rows, :].astype(f32)
        inv = lax.rsqrt(jnp.mean(values * values, axis=-1, keepdims=True) + epsilon)
        values = values * inv * norm_gain[...]
        normed[rows, :] = values.astype(bf16)
        normed_t[:, rows] = jnp.transpose(values).astype(bf16)


def forward_kernel(
    normed,
    seg,
    value_w,
    step_w_t,
    state_w,
    value_conv,
    value_bias,
    state_conv,
    state_bias,
    step_bias,
    decay_log,
    skip_gain,
    y_out,
    u_out,
    p_out,
    bc_out,
    v_out,
    s_out,
    srow_out,
    state_out,
    step_pad,
    heads,
    xd_scratch,
):
    row_count, inner = y_out.shape
    state_size = bc_out.shape[1] // 2
    head_count = step_w_t.shape[0]
    head_size = inner // head_count
    kernel_width = value_conv.shape[0]
    step_pad[...] = jnp.zeros_like(step_pad)
    step_pad[:head_count, :] = step_w_t[...]
    heads[...] = jnp.zeros_like(heads)
    head_rows(step_bias, heads, 0)
    head_rows(decay_log, heads, 1)
    head_rows(skip_gain, heads, 2)
    v = dot(normed[...], step_pad[...], "nt") + heads[0:1, :]
    v_out[...] = v
    dt = softplus(v)
    rate = -jnp.exp(heads[1:2, :])
    spread = head_map(inner, head_size)
    scan = scan_matrix(STRETCH, False)
    for start in range(0, row_count, STRETCH):
        rows = slice(start, start + STRETCH)
        decay = lax.dot_general(
            scan, dt[rows] * rate, (((1,), (0,)), ((), ())), precision=highest,
            preferred_element_type=f32,
        )
        s_out[rows, :] = decay
        srow_out[:, rows] = jnp.transpose(decay)[: srow_out.shape[0]]
    columns = seg_columns(seg)
    masks = delay_masks(columns, kernel_width)
    bc_out[...] = dot(normed[...], state_w[...])
    for start in range(0, 2 * state_size, LANES):
        lanes = slice(start, start + LANES)
        p = conv_chunk(bc_out[:, lanes], masks, state_conv[:, lanes], state_bias[:, lanes])
        bc_out[:, lanes] = p * sigmoid(p)
    u_out[...] = dot(normed[...], value_w[...])
    dt_wide = dot_exact(dt, spread)
    for start in range(0, inner, LANES):
        lanes = slice(start, start + LANES)
        p = conv_chunk(u_out[:, lanes], masks, value_conv[:, lanes], value_bias[:, lanes])
        p_out[:, lanes] = p
        x = p * sigmoid(p)
        xd_scratch[:, lanes] = x * dt_wide[:, lanes]
        skip = dot_exact(heads[...], spread[:, lanes])[2:3]
        y_out[:, lanes] = x * skip
    even = iota((STRETCH, LANES), 1) < head_size
    shape = (STRETCH, STRETCH)
    causal = iota(shape, 0) >= iota(shape, 1)
    seg_row = seg[...].astype(f32)
    for start in range(0, row_count, STRETCH):
        rows = slice(start, start + STRETCH)
        keys = bc_out[rows, :state_size].astype(bf16)
        queries = bc_out[rows, state_size:].astype(bf16)
        same = (columns[rows, 0:1] == seg_row[:, rows]) & causal
        scores = jnp.where(same, dot(queries, keys, "nt"), 0.0)
        for pair in range(inner // LANES):
            lanes = slice(pair * LANES, (pair + 1) * LANES)
            xd = xd_scratch[rows, lanes].astype(bf16)
            found = []
            for head in (2 * pair, 2 * pair + 1):
                gap = s_out[rows, head : head + 1] - srow_out[head : head + 1, rows]
                weight = jnp.exp(jnp.minimum(gap, 0.0)) * scores
                found.append(dot(weight.astype(bf16), xd))
            y_out[rows, lanes] += jnp.where(even, found[0], found[1])
        if start == 0:
            last = columns[STRETCH - 1 : STRETCH, :]
            tail = jnp.where(
                columns[rows] == last,
                jnp.exp(s_out[STRETCH - 1 : STRETCH, :] - s_out[rows, :]),
                0.0,
            )
            tailed = (xd_scratch[rows, :] * dot_exact(tail, spread)).astype(bf16)
            state_out[...] = dot(keys, tailed, "tn")
        else:
            factor = jnp.where(columns[rows] == last, jnp.exp(s_out[rows, :]), 0.0)
            y_out[rows, :] += dot(queries, state_out[...].astype(bf16)) * dot_exact(factor, spread)


def gate_forward_kernel(normed, y, gate_w, cotangent, out_w, gated_gain, z_out, gg_out, rows_out):
    row_count = y.shape[0]
    z_out[...] = dot(normed[...], gate_w[...])
    gg_out[...] = dot(cotangent[...], out_w[...], "nt")
    z = z_out[...]
    gated_in = y[...] * (z * sigmoid(z))
    squares = jnp.sum(gated_in * gated_in, axis=-1, keepdims=True)
    dots = jnp.sum(gg_out[...] * gated_gain[...] * gated_in, axis=-1, keepdims=True)
    lane = iota((row_count, LANES), 1)
    both = jnp.where(lane == 0, squares, jnp.where(lane == 1, dots, 0.0))
    rows_out[...] = jnp.transpose(both)[: rows_out.shape[0]]


def out_grad_kernel(inner_total, order, rows, rows_got, y, z, gated_gain, cotangent, *rest):
    *outs, gated_out, col_out, rows_pad, gated_t = rest
    rows_pad[...] = jnp.zeros_like(rows_pad)
    rows_pad[: rows.shape[0], :] = rows[...] + rows_got[...]
    sums = jnp.transpose(rows_pad[...])
    inv = lax.rsqrt(sums[:, 0:1] / inner_total + epsilon)
    lane = iota(sums.shape, 1)
    col_out[...] = jnp.where(lane == 0, inv, sums)
    zv = z[...]
    gated = (y[...] * (zv * sigmoid(zv))) * inv * gated_gain[...]
    gated_out[...] = gated.astype(bf16)
    gated_t[...] = jnp.transpose(gated).astype(bf16)
    if order is None:
        outs[0][...] = dot(gated_t[...], cotangent[...])
    else:
        me = lax.axis_index("dp")
        keep, send = outs
        half, _, width = keep.shape
        for place, slot in enumerate(order):
            start = pl.multiple_of((me ^ slot) * width, width)
            part = dot(gated_t[...], cotangent[:, pl.ds(start, width)])
            (keep if place < half else send)[place % half] = part


def row_slots(matrix_t, low, keep, send, order, axis):
    me = lax.axis_index(axis)
    half, height, _ = keep.shape
    for place, slot in enumerate(order):
        start = pl.multiple_of((me ^ slot) * height, height)
        part = dot(matrix_t[pl.ds(start, height), :], low)
        (keep if place < half else send)[place % half] = part


def gate_kernel(
    inner_total, order, y, z, gg, gated_gain, col, normed_t, keep, send, gate_low, dy_out, gain_out
):
    inv, dots = col[:, 0:1], col[:, 1:2]
    scale = inv * inv * inv * dots / inner_total
    for start in range(0, y.shape[1], LANES):
        lanes = slice(start, start + LANES)
        zv, yv, ggv = z[:, lanes], y[:, lanes], gg[:, lanes]
        sig = sigmoid(zv)
        silu = zv * sig
        gated_in = yv * silu
        mixer = ggv * gated_gain[:, lanes] * inv - gated_in * scale
        gain_out[:, lanes] = jnp.sum(ggv * gated_in * inv, axis=0, keepdims=True)
        dy_out[:, lanes] = mixer * silu
        gate_low[:, lanes] = (mixer * yv * (sig * (1.0 + zv * (1.0 - sig)))).astype(bf16)
    row_slots(normed_t, gate_low[...], keep, send, order, "dp")


def branch_kernel(order, gated, out_w, keep, send):
    row_slots(gated, out_w[...], keep, send, order, "tensor")


def mixer_back_kernel(
    order,
    head_count,
    dy,
    p,
    bc,
    v,
    s,
    srow,
    state,
    seg,
    decay_log,
    skip_gain,
    dx_out,
    keep,
    send,
    step_low,
    heads_out,
    heads,
    xd_scratch,
    dxd_scratch,
    dbc_t,
    rows_pad,
):
    row_count, inner = dy.shape
    state_size = bc.shape[1] // 2
    head_size = inner // head_count
    heads[...] = jnp.zeros_like(heads)
    head_rows(decay_log, heads, 1)
    head_rows(skip_gain, heads, 2)
    rate = -jnp.exp(heads[1:2, :])
    dt = softplus(v[...])
    spread = head_map(inner, head_size)
    skip_wide = dot_exact(heads[...], spread)[2:3]
    columns = seg_columns(seg)
    seg_row = seg[...].astype(f32)
    last = columns[STRETCH - 1 : STRETCH, :]
    even = iota((STRETCH, LANES), 1) < head_size
    lane = iota((STRETCH, LANES), 1)
    shape = (STRETCH, STRETCH)
    causal_t = iota(shape, 1) >= iota(shape, 0)
    scan = scan_matrix(STRETCH, True)
    dt_wide = dot_exact(dt, spread)
    pv = p[...]
    x = pv * sigmoid(pv)
    xd_scratch[...] = x * dt_wide

    first, second = slice(0, STRETCH), slice(STRETCH, 2 * STRETCH)
    queries = bc[second, state_size:].astype(bf16)
    keys = bc[first, :state_size].astype(bf16)
    state_low = state[...].astype(bf16)
    factor = jnp.where(columns[second] == last, jnp.exp(s[second, :]), 0.0)
    dcarry = dy[second, :] * dot_exact(factor, spread)
    dcarry_low = dcarry.astype(bf16)
    dbc_t[state_size:, second] = dot(state_low, dcarry_low, "nt")
    dstate = dot(queries, dcarry_low, "tn").astype(bf16)
    ds_second = dot_exact(dcarry * dot(queries, state_low), spread, "nt")
    tail = jnp.where(
        columns[first] == last, jnp.exp(s[STRETCH - 1 : STRETCH, :] - s[first, :]), 0.0
    )
    tail_wide = dot_exact(tail, spread)
    tailed = xd_scratch[first, :] * tail_wide
    dbc_t[:state_size, first] = dot(dstate, tailed.astype(bf16), "nt")
    dbc_t[state_size:, first] = jnp.zeros((state_size, STRETCH), f32)
    dbc_t[:state_size, second] = jnp.zeros((state_size, STRETCH), f32)
    dtailed = dot(keys, dstate)
    dxd_scratch[first, :] = dtailed * tail_wide
    dxd_scratch[second, :] = jnp.zeros((STRETCH, inner), f32)
    ds_tail = dot_exact(dtailed * tailed, spread, "nt")
    at = iota((STRETCH, LANES), 0)
    ds_first = jnp.where(at == STRETCH - 1, jnp.sum(ds_tail, axis=0, keepdims=True), 0.0) - ds_tail

    dskip = jnp.zeros((1, LANES), f32)
    ddecay = jnp.zeros((1, LANES), f32)
    dbias = jnp.zeros((1, LANES), f32)
    rows_pad[...] = jnp.zeros_like(rows_pad)
    for rows, ds in ((first, ds_first), (second, ds_second)):
        keys = bc[rows, :state_size].astype(bf16)
        queries = bc[rows, state_size:].astype(bf16)
        same = (columns[rows, 0:1] == seg_row[:, rows]) & causal_t
        scores = jnp.where(same, dot(keys, queries, "nt"), 0.0)
        dscores = jnp.zeros(shape, f32)
        for pair in range(inner // LANES):
            lanes = slice(pair * LANES, (pair + 1) * LANES)
            xd = xd_scratch[rows, lanes].astype(bf16)
            dyv = dy[rows, lanes].astype(bf16)
            found = []
            for place, head in enumerate((2 * pair, 2 * pair + 1)):
                gap = srow[head : head + 1, rows] - s[rows, head : head + 1]
                decay = jnp.exp(jnp.minimum(gap, 0.0))
                mine = even if place == 0 else jnp.logical_not(even)
                cross = dot(jnp.where(mine, xd, jnp.zeros_like(xd)), dyv, "nt")
                weight = decay * scores
                dscores = dscores + decay * cross
                moved = weight * cross
                ds = ds - jnp.where(lane == head, jnp.sum(moved, axis=1, keepdims=True), 0.0)
                rows_pad[head : head + 1, :] = jnp.sum(moved, axis=0, keepdims=True)
                found.append(dot(weight.astype(bf16), dyv))
            dxd_scratch[rows, lanes] += jnp.where(even, found[0], found[1])
        dscores = jnp.where(same, dscores, 0.0).astype(bf16)
        dbc_t[:state_size, rows] += dot(jnp.transpose(queries), dscores, "nt")
        dbc_t[state_size:, rows] += dot(jnp.transpose(keys), dscores)
        ds = ds + jnp.transpose(rows_pad[...])
        da = lax.dot_general(
            scan, ds, (((1,), (0,)), ((), ())), precision=highest, preferred_element_type=f32
        )
        pv = p[rows, :]
        x = pv * sigmoid(pv)
        dxd = dxd_scratch[rows, :]
        dyv = dy[rows, :]
        ddt = dot_exact(dxd * x, spread, "nt") + da * rate
        dx_out[rows, :] = dxd * dt_wide[rows] + dyv * skip_wide
        dstep = ddt * sigmoid(v[rows, :])
        step_low[rows, :] = dstep.astype(bf16)
        dbias = dbias + jnp.sum(dstep, axis=0, keepdims=True)
        ddecay = ddecay + jnp.sum(da * dt[rows], axis=0, keepdims=True)
        dskip = dskip + dot_exact(jnp.sum(dyv * x, axis=0, keepdims=True) + jnp.zeros((8, 1), f32), spread, "nt")[0:1]
    heads_out[...] = jnp.zeros_like(heads_out)
    heads_out[0:1, :] = dbias
    heads_out[1:2, :] = ddecay * rate
    heads_out[2:3, :] = dskip
    me = lax.axis_index("tensor")
    half, height, _ = keep.shape
    for place, slot in enumerate(order):
        start = pl.multiple_of((me ^ slot) * height, height)
        (keep if place < half else send)[place % half] = dbc_t[pl.ds(start, height), :]


def value_kernel(order, dx, p, u, seg, value_conv, normed_t, keep, send, value_low, small):
    kernel_width = value_conv.shape[0]
    masks = delay_masks(seg_columns(seg), kernel_width)
    row_count, inner = dx.shape
    small[...] = jnp.zeros_like(small)
    for start in range(0, inner, LANES):
        lanes = slice(start, start + LANES)
        pv, uv = p[:, lanes], u[:, lanes]
        sig = sigmoid(pv)
        gp = dx[:, lanes] * (sig * (1.0 + pv * (1.0 - sig)))
        du = value_conv[kernel_width - 1 :, lanes] * gp
        small[kernel_width - 1 : kernel_width, lanes] = jnp.sum(gp * uv, axis=0, keepdims=True)
        small[kernel_width : kernel_width + 1, lanes] = jnp.sum(gp, axis=0, keepdims=True)
        for delay, mask in masks.items():
            tap = kernel_width - 1 - delay
            masked = gp * mask
            du = du + value_conv[tap : tap + 1, lanes] * pltpu.roll(masked, row_count - delay, 0)
            small[tap : tap + 1, lanes] = jnp.sum(
                masked * pltpu.roll(uv, delay, 0), axis=0, keepdims=True
            )
        value_low[:, lanes] = du.astype(bf16)
    row_slots(normed_t, value_low[...], keep, send, order, "dp")


def normed_kernel(
    dp_order,
    order,
    states_keep,
    states_got,
    states_last,
    normed_t,
    state_w,
    state_conv,
    state_bias,
    seg,
    gate_low,
    value_low,
    step_low,
    gate_w,
    value_w,
    step_w_t,
    tokens,
    small,
    gain_row,
    heads,
    keep,
    send,
    nk_keep,
    nk_send,
    step_pad,
    raw_t,
    conv_pad,
    conv_t,
    low_full,
    narrow_full,
    total,
    packed,
):
    kernel_width = state_conv.shape[0]
    head_count = step_w_t.shape[0]
    _, own, row_count = states_keep.shape
    model_width = state_w.shape[0]
    rank = lax.axis_index("tensor")
    own_rows = pl.ds(pl.multiple_of(rank * own, own), own)
    step_pad[...] = jnp.zeros_like(step_pad)
    step_pad[:head_count, :] = step_w_t[...]
    raw_t[...] = dot(state_w[...], normed_t[...], "tn")
    conv_pad[...] = jnp.zeros_like(conv_pad)
    conv_pad[:kernel_width, :] = state_conv[...]
    conv_pad[kernel_width : kernel_width + 1, :] = state_bias[...]
    conv_t[...] = jnp.transpose(conv_pad[...])
    raw = raw_t[own_rows, :]
    conv = conv_t[own_rows, :]
    seg_row = jnp.broadcast_to(seg[...].astype(f32), (8, row_count))
    at = iota((8, row_count), 1)
    p = conv[:, kernel_width : kernel_width + 1] + conv[:, kernel_width - 1 : kernel_width] * raw
    masks = {}
    for delay in range(1, kernel_width):
        tap = kernel_width - 1 - delay
        mask = jnp.where((pltpu.roll(seg_row, delay, 1) == seg_row) & (at >= delay), 1.0, 0.0)
        masks[delay] = mask[0:1]
        p = p + conv[:, tap : tap + 1] * (pltpu.roll(raw, delay, 1) * masks[delay])
    sig = sigmoid(p)
    gp = (states_keep[0] + states_got[0] + states_last[0]) * (sig * (1.0 + p * (1.0 - sig)))
    du = conv[:, kernel_width - 1 : kernel_width] * gp
    lane = iota((own, LANES), 1)

    def put(column, value):
        return jnp.where(lane == column, jnp.sum(value, axis=1, keepdims=True), 0.0)

    grads = put(kernel_width - 1, gp * raw) + put(kernel_width, gp)
    for delay, mask in masks.items():
        tap = kernel_width - 1 - delay
        masked = gp * mask
        du = du + conv[:, tap : tap + 1] * pltpu.roll(masked, row_count - delay, 1)
        grads = grads + put(tap, masked * pltpu.roll(raw, delay, 1))
    state_low = du.astype(bf16)
    narrow_full[:own, :] = dot(state_low, normed_t[...], "nt")
    step_rows = jnp.transpose(step_low[...].astype(f32))[:head_count].astype(bf16)
    narrow_full[own:, :] = dot(step_rows, normed_t[...], "nt")
    low_full[...] = jnp.zeros_like(low_full)
    low_full[own_rows, :] = state_low
    total[...] = dot(gate_low[...], gate_w[...], "nt")
    total[...] += dot(value_low[...], value_w[...], "nt")
    total[...] += dot(step_low[...], step_pad[...])
    total[...] += dot(
        jnp.transpose(low_full[...].astype(f32)).astype(bf16), state_w[...], "nt"
    )
    part = jnp.zeros((1, model_width), f32)
    for start in range(0, row_count, LANES):
        rows = slice(start, start + LANES)
        values = tokens[rows, :].astype(f32)
        inv = lax.rsqrt(jnp.mean(values * values, axis=-1, keepdims=True) + epsilon)
        part = part + jnp.sum(total[rows, :] * (values * inv), axis=0, keepdims=True)
    inner = packed.shape[1]
    packed[...] = jnp.zeros_like(packed)
    packed[: kernel_width + 1, :] = small[: kernel_width + 1, :]
    base = kernel_width + 1
    packed[base : base + 1, :] = gain_row[...]
    for start in range(0, model_width, inner):
        base += 1
        packed[base : base + 1, :] = part[:, start : start + inner]
    base += 1
    packed[base : base + 3, :LANES] = heads[0:3, :]
    height = own + head_count
    if dp_order is None:
        nk_keep[...] = narrow_full[...]
        at_row = 0
    else:
        me = lax.axis_index("dp")
        half = len(dp_order) // 2
        for place, slot in enumerate(dp_order):
            start = pl.multiple_of((me ^ slot) * LANES, LANES)
            rows = pl.ds(place % half * height, height)
            (nk_keep if place < half else nk_send)[rows, :] = narrow_full[:, pl.ds(start, LANES)]
        at_row = half * height
    for start in range(0, inner, LANES):
        nk_send[at_row : at_row + 16, :] = packed[:, start : start + LANES]
        at_row += 16
    nk_send[at_row : at_row + own, :] = grads
    half, height, _ = keep.shape
    for place, slot in enumerate(order):
        start = pl.multiple_of((rank ^ slot) * height, height)
        (keep if place < half else send)[place % half] = total[pl.ds(start, height), :]


def small_step_kernel(keep, sent, got, keep_out, send_out):
    count, half = keep.shape[0], keep_out.shape[0]
    keep_out[...] = keep[:half, :] + got[:half, :]
    send_out[:half, :] = keep[half:, :] + got[half:count, :]
    send_out[half:, :] = sent[count:, :] + got[count:, :]


def small_layout(kernel_width, inner, model_width):
    gain = kernel_width + 1
    norm = gain + 1
    heads = norm + model_width // inner
    return gain, norm, heads


def small_last_kernel(layout, own, inner, keep, sent, got, narrow, sums, share):
    count = keep.shape[0]
    narrow[...] = keep[...] + got[:count, :]
    sums[...] = sent[count:, :] + got[count:, :]
    share[:own, :] = narrow[:own, :]
    share[own : 2 * own, :] = sums[sums.shape[0] - own :, :]
    _, norm, heads = layout
    at = 2 * own
    for row in range(norm, heads):
        for group in range(inner // LANES):
            share[at : at + 1, :] = sums[16 * group + row : 16 * group + row + 1, :]
            at += 1


def finish_kernel(layout, own, parts, *refs):
    shares, (narrow, sums), refs = refs[:parts], refs[parts : parts + 2], refs[parts + 2 :]
    *outs, states, convs = refs
    norm_o, vconv_o, vbias_o, sconv_o, sbias_o, sb_o, dl_o, sk_o, gain_o, step_o, state_o = outs
    gain, norm, heads = layout
    kernel_width, inner = vconv_o.shape
    rank = lax.axis_index("tensor")
    for slot, share in enumerate(shares):
        rows = pl.ds(pl.multiple_of((rank ^ slot) * own, own), own)
        states[rows, :] = share[:own, :]
        convs[rows, :] = share[own : 2 * own, :]
    state_o[...] = jnp.transpose(states[...])
    turned = jnp.transpose(convs[...])
    sconv_o[...] = turned[:kernel_width]
    sbias_o[...] = turned[kernel_width : kernel_width + 1]
    step_o[...] = narrow[own:, :]
    total = shares[0][2 * own :, :]
    for share in shares[1:]:
        total = total + share[2 * own :, :]
    for place in range(total.shape[0]):
        norm_o[:, place * LANES : (place + 1) * LANES] = total[place : place + 1]
    for group in range(inner // LANES):
        lanes = slice(group * LANES, (group + 1) * LANES)
        block = sums[16 * group : 16 * group + 16, :]
        vconv_o[:, lanes] = block[:kernel_width]
        vbias_o[:, lanes] = block[kernel_width : kernel_width + 1]
        gain_o[:, lanes] = block[gain : gain + 1]
        if group == 0:
            for place, out in enumerate((sb_o, dl_o, sk_o)):
                out[...] = block[heads + place : heads + place + 1, : out.shape[1]]


def own_share(whole, scratch, sem):
    height = scratch.shape[0]
    start = pl.multiple_of(lax.axis_index("tensor") * height, height)
    return pltpu.make_async_copy(whole.at[pl.ds(start, height), :], scratch, sem)


def tokens_kernel(keep, got, last, norm_gain, tokens, cotangent, out, mine, theirs, sems):
    first, second = own_share(tokens, mine, sems.at[0]), own_share(cotangent, theirs, sems.at[1])
    first.start()
    second.start()
    first.wait()
    second.wait()
    model_width = tokens.shape[1]
    grad = keep[0] + got[0] + last[0]
    values = mine[...].astype(f32)
    inv = lax.rsqrt(jnp.mean(values * values, axis=-1, keepdims=True) + epsilon)
    scaled = grad * norm_gain[...]
    sums = jnp.sum(scaled * values, axis=-1, keepdims=True)
    out[...] = (
        scaled * inv
        - values * (inv * inv * inv) * sums / model_width
        + theirs[...].astype(f32)
    ).astype(bf16)


def mixed_kernel(keep, got, last, tokens, out, mine, sem):
    copy = own_share(tokens, mine, sem)
    copy.start()
    copy.wait()
    out[...] = (mine[...].astype(f32) + (keep[0] + got[0] + last[0])).astype(bf16)


def call(kernel, outs, args, scratch=(), name=None, cost=None, whole=0):
    vmem = pl.BlockSpec(memory_space=pltpu.VMEM)
    return pl.pallas_call(
        kernel,
        name=name,
        out_shape=[jax.ShapeDtypeStruct(shape, kind) for shape, kind in outs],
        in_specs=[vmem] * (len(args) - whole) + [pl.BlockSpec(memory_space=pl.ANY)] * whole,
        out_specs=[vmem] * len(outs),
        scratch_shapes=[
            piece if callable(getattr(piece, "get_array_aval", None)) else pltpu.VMEM(*piece)
            for piece in scratch
        ],
        compiler_params=pltpu.CompilerParams(vmem_limit_bytes=VMEM_LIMIT),
        cost_estimate=cost,
    )(*args)


def cost(flops, moved):
    return pl.CostEstimate(flops=int(flops), bytes_accessed=int(moved), transcendentals=0)


def body(
    tokens,
    cotangent,
    segment,
    norm_gain,
    gate_weight,
    value_weight,
    step_weight,
    state_weight,
    value_conv,
    value_conv_bias,
    state_conv,
    state_conv_bias,
    step_bias,
    decay_log,
    skip_gain,
    gated_gain,
    out_weight,
):
    row_count, model_width = tokens.shape
    tensor_parts = lax.axis_size("tensor")
    dp_parts = lax.axis_size("dp")
    share = row_count // tensor_parts
    heads_here = step_weight.shape[1]
    inner = gate_weight.shape[1]
    inner_total = inner * tensor_parts
    state_width = state_weight.shape[1]
    state_size = state_width // 2
    own_states = state_width // tensor_parts
    kernel_width = value_conv.shape[0]
    tensor_bits, dp_bits = bits_of(tensor_parts), bits_of(dp_parts)
    near_bits, far_bits = dp_bits, dp_bits[1:] + dp_bits[:1]
    tensor_order = slot_order(tensor_bits)
    near_order, far_order = slot_order(near_bits), slot_order(far_bits)
    shard = model_width // dp_parts
    aligned = shard % LANES == 0
    assert row_count == SEQ_LEN == 2 * STRETCH and inner // heads_here * 2 == LANES

    def row(array):
        return array.reshape(1, -1)

    seg = row(segment)
    step_t = step_weight.T
    normed, normed_t = call(
        norm_kernel,
        [((row_count, model_width), bf16), ((model_width, row_count), bf16)],
        [tokens, row(norm_gain)],
        name="norm",
        cost=cost(1e6, 3e6),
    )
    y, u, p, bc, v, s, srow, state = call(
        forward_kernel,
        [
            ((row_count, inner), f32),
            ((row_count, inner), f32),
            ((row_count, inner), f32),
            ((row_count, state_width), f32),
            ((row_count, LANES), f32),
            ((row_count, LANES), f32),
            ((heads_here, row_count), f32),
            ((state_size, inner), f32),
        ],
        [
            normed,
            seg,
            value_weight,
            step_t,
            state_weight,
            value_conv,
            row(value_conv_bias),
            state_conv,
            row(state_conv_bias),
            row(step_bias),
            row(decay_log),
            row(skip_gain),
        ],
        [
            ((LANES, model_width), bf16),
            ((8, LANES), f32),
            ((row_count, inner), f32),
        ],
        name="forward",
        cost=cost(3e9, 10e6),
    )
    z, gg, rows = call(
        gate_forward_kernel,
        [((row_count, inner), f32), ((row_count, inner), f32), ((8, row_count), f32)],
        [normed, y, gate_weight, cotangent, out_weight, row(gated_gain)],
        name="gate_forward",
        cost=cost(2e9, 6e6),
    )
    for bit in tensor_bits[:-1]:
        with jax.named_scope(f"rows{bit}"):
            rows = rows + swap(rows, "tensor", bit)
    with jax.named_scope("rowslast"):
        rows_got = swap(rows, "tensor", tensor_bits[-1])

    half = dp_parts // 2
    if aligned:
        out_shapes = [((half, inner, shard), f32)] * 2
    else:
        out_shapes = [((inner, model_width), f32)]
    *out_pair, gated, col = call(
        partial(out_grad_kernel, inner_total, near_order if aligned else None),
        out_shapes + [((row_count, inner), bf16), ((row_count, LANES), f32)],
        [rows, rows_got, y, z, row(gated_gain), cotangent],
        [((LANES, row_count), f32), ((inner, row_count), bf16)],
        name="out_grad",
        cost=cost(1e9, 6e6),
    )
    if aligned:
        grad_out_shard = halving(*out_pair, "dp", near_bits, "o")
    else:
        split = out_pair[0].reshape(inner, dp_parts, shard)
        grad_out_shard = scatter_sum(jnp.swapaxes(split, 0, 1), "dp", dp_bits)
    weight_slots = [((half, shard, inner), f32)] * 2
    gate_keep, gate_send, gate_low, dy, gain_row = call(
        partial(gate_kernel, inner_total, far_order),
        weight_slots + [((row_count, inner), bf16), ((row_count, inner), f32), ((1, inner), f32)],
        [y, z, gg, row(gated_gain), col, normed_t],
        name="gate_grad",
        cost=cost(1e9, 7e6),
    )
    gate_shard = halving(gate_keep, gate_send, "dp", far_bits, "g")
    row_shares = [((tensor_parts // 2, share, model_width), f32)] * 2
    branch_keep, branch_send = call(
        partial(branch_kernel, tensor_order),
        row_shares,
        [gated, out_weight],
        name="branch",
        cost=cost(1e9, 4e6),
    )
    dx, states_keep, states_send, step_low, head_sums = call(
        partial(mixer_back_kernel, tensor_order, heads_here),
        [
            ((row_count, inner), f32),
            ((tensor_parts // 2, own_states, row_count), f32),
            ((tensor_parts // 2, own_states, row_count), f32),
            ((row_count, LANES), bf16),
            ((8, LANES), f32),
        ],
        [dy, p, bc, v, s, srow, state, seg, row(decay_log), row(skip_gain)],
        [
            ((8, LANES), f32),
            ((row_count, inner), f32),
            ((row_count, inner), f32),
            ((state_width, row_count), f32),
            ((LANES, STRETCH), f32),
        ],
        name="mixer_back",
        cost=cost(6e9, 8e6),
    )
    states = halving_parts(states_keep, states_send, "tensor", tensor_bits, "s")
    value_keep, value_send, value_low, small = call(
        partial(value_kernel, near_order),
        weight_slots + [((row_count, inner), bf16), ((8, inner), f32)],
        [dx, p, u, seg, value_conv, normed_t],
        name="value_grad",
        cost=cost(2e9, 7e6),
    )
    value_shard = halving(value_keep, value_send, "dp", near_bits, "v")
    narrow_rows = own_states + heads_here
    group_rows = 16 * (inner // LANES)
    if aligned:
        small_shapes = [
            ((half * narrow_rows, LANES), f32),
            ((half * narrow_rows + group_rows + own_states, LANES), f32),
        ]
    else:
        small_shapes = [
            ((narrow_rows, model_width), f32),
            ((group_rows + own_states, LANES), f32),
        ]
    normed_keep, normed_send, small_keep, small_send = call(
        partial(normed_kernel, far_order if aligned else None, tensor_order),
        row_shares + small_shapes,
        [
            *states,
            normed_t,
            state_weight,
            state_conv,
            row(state_conv_bias),
            seg,
            gate_low,
            value_low,
            step_low,
            gate_weight,
            value_weight,
            step_t,
            tokens,
            small,
            gain_row,
            head_sums,
        ],
        [
            ((LANES, model_width), bf16),
            ((state_width, row_count), f32),
            ((LANES, state_width), f32),
            ((state_width, LANES), f32),
            ((state_width, row_count), bf16),
            ((narrow_rows, model_width), f32),
            ((row_count, model_width), f32),
            ((16, inner), f32),
        ],
        name="normed_grad",
        cost=cost(4e9, 10e6),
    )
    normed_terms = halving_parts(normed_keep, normed_send, "tensor", tensor_bits, "n")
    (grad_tokens,) = call(
        tokens_kernel,
        [((share, model_width), bf16)],
        [*normed_terms, row(norm_gain), tokens, cotangent],
        [((share, model_width), bf16)] * 2 + [pltpu.SemaphoreType.DMA((2,))],
        name="token_grad",
        cost=cost(1e6, 2e6),
        whole=2,
    )
    branch_terms = halving_parts(branch_keep, branch_send, "tensor", tensor_bits, "b")
    (mixed,) = call(
        mixed_kernel,
        [((share, model_width), bf16)],
        [*branch_terms, tokens],
        [((share, model_width), bf16), pltpu.SemaphoreType.DMA(())],
        name="mixed",
        cost=cost(1e6, 2e6),
        whole=1,
    )

    layout = small_layout(kernel_width, inner, model_width)
    sums_shape = ((group_rows + own_states, LANES), f32)
    share_rows = 2 * own_states + model_width // LANES
    last_shapes = [((narrow_rows, LANES), f32), sums_shape, ((share_rows, LANES), f32)]
    if aligned:
        count = half
        for step, bit in enumerate(far_bits):
            with jax.named_scope(f"k{step}"):
                small_got = swap(small_send, "dp", bit)
            if count > 1:
                count //= 2
                small_keep, small_send = call(
                    small_step_kernel,
                    [
                        ((count * narrow_rows, LANES), f32),
                        ((count * narrow_rows + sums_shape[0][0], LANES), f32),
                    ],
                    [small_keep, small_send, small_got],
                    name=f"small{step}",
                    cost=cost(1e6, 1e6),
                )
    else:
        split = small_keep.reshape(narrow_rows, dp_parts, shard)
        narrow = scatter_sum(jnp.swapaxes(split, 0, 1), "dp", dp_bits)
        small_keep = jnp.pad(narrow, ((0, 0), (0, LANES - shard)))
        sums = all_sum(small_send, "dp")
        small_send = jnp.concatenate([jnp.zeros_like(small_keep), sums])
        small_got = jnp.zeros_like(small_send)
    narrow, sums, shared = call(
        partial(small_last_kernel, layout, own_states, inner),
        last_shapes,
        [small_keep, small_send, small_got],
        name="small_last",
        cost=cost(1e6, 1e6),
    )
    shares = [shared]
    for slot in range(1, tensor_parts):
        with jax.named_scope(f"t{slot}"):
            shares.append(swap(shared, "tensor", slot))
    one = (1, inner)
    head_row = ((1, heads_here), f32)
    (
        norm_row,
        value_taps,
        value_bias,
        state_taps,
        state_bias,
        step_bias_row,
        decay_row,
        skip_row,
        gain_sum,
        step_grad,
        state_grad,
    ) = call(
        partial(finish_kernel, layout, own_states, tensor_parts),
        [
            ((1, model_width), f32),
            (value_conv.shape, f32),
            (one, f32),
            (state_conv.shape, f32),
            ((1, state_width), f32),
            head_row,
            head_row,
            head_row,
            (one, f32),
            ((heads_here, LANES), f32),
            ((LANES, state_width), f32),
        ],
        [*shares, narrow, sums],
        [((state_width, LANES), f32)] * 2,
        name="finish",
        cost=cost(1e6, 1e6),
    )
    return (
        mixed,
        grad_tokens,
        norm_row.reshape(-1),
        gate_shard,
        value_shard,
        step_grad[:, :shard].T,
        state_grad[:shard],
        value_taps,
        value_bias.reshape(-1),
        state_taps,
        state_bias.reshape(-1),
        step_bias_row.reshape(-1),
        decay_row.reshape(-1),
        skip_row.reshape(-1),
        gain_sum.reshape(-1),
        grad_out_shard,
    )


def solution(mesh):
    return jax.shard_map(
        body,
        mesh=mesh,
        in_specs=(
            P("dp", None),
            P("dp", None),
            P("dp"),
            P(),
            P(None, "tensor"),
            P(None, "tensor"),
            P(None, "tensor"),
            P(),
            P(None, "tensor"),
            P("tensor"),
            P(),
            P(),
            P("tensor"),
            P("tensor"),
            P("tensor"),
            P("tensor"),
            P("tensor", None),
        ),
        out_specs=(
            P(("dp", "tensor"), None),
            P(("dp", "tensor"), None),
            P(),
            P("dp", "tensor"),
            P("dp", "tensor"),
            P("dp", "tensor"),
            P("dp", None),
            P(None, "tensor"),
            P("tensor"),
            P(),
            P(),
            P("tensor"),
            P("tensor"),
            P("tensor"),
            P("tensor"),
            P("tensor", "dp"),
        ),
        check_vma=False,
    )
```

```python
from functools import partial

import jax
import jax.numpy as jnp
from jax import lax
from jax.experimental import pallas as pl
from jax.experimental.pallas import tpu as pltpu
from jax.sharding import PartitionSpec as P


STRETCH = 256
SEQ_LEN = 512


epsilon = 1e-05
highest = lax.Precision.HIGHEST
f32, bf16 = jnp.float32, jnp.bfloat16
LANES = 128
VMEM_LIMIT = 20 * 2**20
WAYS = {"o": "ynf", "g": "nyf", "va": "ynf", "vb": "ynf", "k": "nfy"}


def swap(array, axis, bit):
    size = lax.axis_size(axis)
    return lax.ppermute(array, axis, [(i, i ^ bit) for i in range(size)])


def bits_of(size):
    assert size & (size - 1) == 0
    return [1 << i for i in range(size.bit_length() - 1)]


def slot_order(bits):
    order = [0]
    for bit in reversed(bits):
        order = order + [slot | bit for slot in order]
    return order


def arranged(bits, way):
    parts = {"y": bits[:1], "n": bits[1:2], "f": bits[2:]}
    return [bit for name in way for bit in parts[name]]


def halving_parts(keep, send, axis, bits):
    terms, size = [keep], keep.shape[0]
    for bit in bits:
        terms.append(swap(send, axis, bit))
        half = size // 2
        if half:
            send = sum(term[half:size] for term in terms[1:]) + keep[half:size]
        size = half
    return terms


def halving(keep, send, axis, bits):
    terms = halving_parts(keep, send, axis, bits)
    first, *rest = [term[0] for term in terms]
    return first + sum(rest)


def scatter_sum(pieces, axis, bits):
    me = lax.axis_index(axis)
    slots = [lax.dynamic_index_in_dim(pieces, me ^ slot, 0) for slot in slot_order(bits)]
    half = len(slots) // 2
    return halving(jnp.concatenate(slots[:half]), jnp.concatenate(slots[half:]), axis, bits)


def all_sum(array, axis):
    for bit in bits_of(lax.axis_size(axis)):
        array = array + swap(array, axis, bit)
    return array


def dot(left, right, form="nn"):
    dims = {"nn": ((1,), (0,)), "nt": ((1,), (1,)), "tn": ((0,), (0,))}[form]
    return lax.dot_general(left, right, (dims, ((), ())), preferred_element_type=f32)


def dot_exact(left, right, form="nn"):
    high = left.astype(bf16)
    low = (left - high.astype(f32)).astype(bf16)
    return dot(high, right, form) + dot(low, right, form)


def sigmoid(v):
    return 1.0 / (1.0 + jnp.exp(-v))


def softplus(v):
    return jnp.maximum(v, 0.0) + jnp.log1p(jnp.exp(-jnp.abs(v)))


def iota(shape, dim):
    return lax.broadcasted_iota(jnp.int32, shape, dim)


def head_map(width, head_size):
    shape = (LANES, width)
    return jnp.where(iota(shape, 0) == iota(shape, 1) // head_size, 1.0, 0.0).astype(bf16)


def seg_columns(seg_ref):
    row = seg_ref[...]
    return jnp.transpose(jnp.broadcast_to(row, (LANES, row.shape[1])))


def delay_masks(columns, kernel_width):
    at = iota(columns.shape, 0)
    return {
        delay: jnp.where((pltpu.roll(columns, delay, 0) == columns) & (at >= delay), 1.0, 0.0)
        for delay in range(1, kernel_width)
    }


def scan_matrix(size, upper):
    shape = (size, size)
    row, column = iota(shape, 0), iota(shape, 1)
    return jnp.where(column >= row if upper else column <= row, 1.0, 0.0)


def conv_chunk(raw, masks, taps, bias):
    kernel_width = taps.shape[0]
    summed = bias + taps[kernel_width - 1 :] * raw
    for delay, mask in masks.items():
        tap = kernel_width - 1 - delay
        summed = summed + taps[tap : tap + 1] * (pltpu.roll(raw, delay, 0) * mask)
    return summed


def norm_kernel(params, tokens, normed, normed_t, seg_out):
    kernel_width = params.shape[0] - 20
    row_count, model_width = tokens.shape
    first = kernel_width + 2
    gain_rows = range(first, first + model_width // params.shape[1])
    gain = jnp.concatenate([params[row : row + 1, :] for row in gain_rows], axis=1)
    seg_out[...] = params[17 + kernel_width : 18 + kernel_width, :row_count]
    for start in range(0, row_count, LANES):
        rows = slice(start, start + LANES)
        values = tokens[rows, :].astype(f32)
        inv = lax.rsqrt(jnp.mean(values * values, axis=-1, keepdims=True) + epsilon)
        values = values * inv * gain
        normed[rows, :] = values.astype(bf16)
        normed_t[:, rows] = jnp.transpose(values).astype(bf16)


def forward_kernel(
    normed,
    seg,
    value_w,
    step_w_t,
    state_w,
    params,
    y_out,
    u_out,
    p_out,
    bc_out,
    v_out,
    s_out,
    srow_out,
    state_out,
    step_pad,
    xd_scratch,
):
    row_count, inner = y_out.shape
    state_size = bc_out.shape[1] // 2
    head_count = step_w_t.shape[0]
    head_size = inner // head_count
    kernel_width = params.shape[0] - 20
    value_conv, value_bias = params[:kernel_width], params[kernel_width : kernel_width + 1]
    state_conv = params[16 : 16 + kernel_width, : 2 * state_size]
    state_bias = params[16 + kernel_width : 17 + kernel_width, : 2 * state_size]
    heads = params[8:16, :LANES]
    step_pad[...] = jnp.zeros_like(step_pad)
    step_pad[:head_count, :] = step_w_t[...]
    v = dot(normed[...], step_pad[...], "nt") + heads[0:1, :]
    v_out[...] = v
    dt = softplus(v)
    rate = -jnp.exp(heads[1:2, :])
    spread = head_map(inner, head_size)
    scan = scan_matrix(STRETCH, False)
    for start in range(0, row_count, STRETCH):
        rows = slice(start, start + STRETCH)
        decay = lax.dot_general(
            scan, dt[rows] * rate, (((1,), (0,)), ((), ())), precision=highest,
            preferred_element_type=f32,
        )
        s_out[rows, :] = decay
        srow_out[:, rows] = jnp.transpose(decay)[: srow_out.shape[0]]
    columns = seg_columns(seg)
    masks = delay_masks(columns, kernel_width)
    bc_out[...] = dot(normed[...], state_w[...])
    for start in range(0, 2 * state_size, LANES):
        lanes = slice(start, start + LANES)
        p = conv_chunk(bc_out[:, lanes], masks, state_conv[:, lanes], state_bias[:, lanes])
        bc_out[:, lanes] = p * sigmoid(p)
    u_out[...] = dot(normed[...], value_w[...])
    dt_wide = dot_exact(dt, spread)
    for start in range(0, inner, LANES):
        lanes = slice(start, start + LANES)
        p = conv_chunk(u_out[:, lanes], masks, value_conv[:, lanes], value_bias[:, lanes])
        p_out[:, lanes] = p
        x = p * sigmoid(p)
        xd_scratch[:, lanes] = x * dt_wide[:, lanes]
        skip = dot_exact(heads, spread[:, lanes])[2:3]
        y_out[:, lanes] = x * skip
    even = iota((STRETCH, LANES), 1) < head_size
    shape = (STRETCH, STRETCH)
    causal = iota(shape, 0) >= iota(shape, 1)
    seg_row = seg[...]
    for start in range(0, row_count, STRETCH):
        rows = slice(start, start + STRETCH)
        keys = bc_out[rows, :state_size].astype(bf16)
        queries = bc_out[rows, state_size:].astype(bf16)
        same = (columns[rows, 0:1] == seg_row[:, rows]) & causal
        scores = jnp.where(same, dot(queries, keys, "nt"), 0.0)
        for pair in range(inner // LANES):
            lanes = slice(pair * LANES, (pair + 1) * LANES)
            xd = xd_scratch[rows, lanes].astype(bf16)
            found = []
            for head in (2 * pair, 2 * pair + 1):
                gap = s_out[rows, head : head + 1] - srow_out[head : head + 1, rows]
                weight = jnp.exp(jnp.minimum(gap, 0.0)) * scores
                found.append(dot(weight.astype(bf16), xd))
            y_out[rows, lanes] += jnp.where(even, found[0], found[1])
        if start == 0:
            last = columns[STRETCH - 1 : STRETCH, :]
            tail = jnp.where(
                columns[rows] == last,
                jnp.exp(s_out[STRETCH - 1 : STRETCH, :] - s_out[rows, :]),
                0.0,
            )
            tailed = (xd_scratch[rows, :] * dot_exact(tail, spread)).astype(bf16)
            state_out[...] = dot(keys, tailed, "tn")
        else:
            factor = jnp.where(columns[rows] == last, jnp.exp(s_out[rows, :]), 0.0)
            y_out[rows, :] += dot(queries, state_out[...].astype(bf16)) * dot_exact(factor, spread)


def gate_forward_kernel(normed, y, gate_w, cotangent, out_w, params, z_out, gg_out, rows_out):
    row_count = y.shape[0]
    gated_gain = gain_of(params)
    z_out[...] = dot(normed[...], gate_w[...])
    gg_out[...] = dot(cotangent[...], out_w[...], "nt")
    z = z_out[...]
    gated_in = y[...] * (z * sigmoid(z))
    squares = jnp.sum(gated_in * gated_in, axis=-1, keepdims=True)
    dots = jnp.sum(gg_out[...] * gated_gain * gated_in, axis=-1, keepdims=True)
    lane = iota((row_count, LANES), 1)
    both = jnp.where(lane == 0, squares, jnp.where(lane == 1, dots, 0.0))
    rows_out[...] = jnp.transpose(both)[: rows_out.shape[0]]


def gain_of(params):
    row = params.shape[0] - 19
    return params[row : row + 1, :]


def scaled_kernel(y, z, params, scaled_t):
    zv = z[...]
    scaled_t[...] = jnp.transpose((y[...] * (zv * sigmoid(zv))) * gain_of(params))


def column_parts(matrix_t, columns, out, slots, axis):
    if slots is None:
        out[...] = dot(matrix_t, columns[...])
        return
    me = lax.axis_index(axis)
    width = out.shape[2]
    for place, slot in enumerate(slots):
        start = pl.multiple_of((me ^ slot) * width, width)
        out[place] = dot(matrix_t, columns[:, pl.ds(start, width)])


def row_parts(matrix_t, low, out, slots, axis):
    me = lax.axis_index(axis)
    height = out.shape[1]
    for place, slot in enumerate(slots):
        start = pl.multiple_of((me ^ slot) * height, height)
        out[place] = dot(matrix_t[pl.ds(start, height), :], low)


def out_send_kernel(inner_total, slots, rows, rows_got, scaled_t, cotangent, send, gated_t):
    inv = lax.rsqrt((rows[0:1, :] + rows_got[0:1, :]) / inner_total + epsilon)
    gated_t[...] = (scaled_t[...] * inv).astype(bf16)
    column_parts(gated_t[...], cotangent, send, slots, "dp")


def gate_send_kernel(
    inner_total,
    slots,
    rows,
    rows_got,
    y,
    z,
    gg,
    params,
    normed_t,
    send,
    gate_low,
    dy_out,
    gain_out,
    rows_pad,
):
    rows_pad[...] = jnp.zeros_like(rows_pad)
    rows_pad[: rows.shape[0], :] = rows[...] + rows_got[...]
    col = jnp.transpose(rows_pad[...])
    inv = lax.rsqrt(col[:, 0:1] / inner_total + epsilon)
    scale = inv * inv * inv * col[:, 1:2] / inner_total
    gated_gain = gain_of(params)
    for start in range(0, y.shape[1], LANES):
        lanes = slice(start, start + LANES)
        zv, yv, ggv = z[:, lanes], y[:, lanes], gg[:, lanes]
        sig = sigmoid(zv)
        silu = zv * sig
        gated_in = yv * silu
        mixer = ggv * gated_gain[:, lanes] * inv - gated_in * scale
        gain_out[:, lanes] = jnp.sum(ggv * gated_in * inv, axis=0, keepdims=True)
        dy_out[:, lanes] = mixer * silu
        gate_low[:, lanes] = (mixer * yv * (sig * (1.0 + zv * (1.0 - sig)))).astype(bf16)
    row_parts(normed_t, gate_low[...], send, slots, "dp")


def keep_kernel(
    out_slots,
    gate_slots,
    value_slots,
    order,
    gated_t,
    cotangent,
    normed_t,
    gate_low,
    value_low,
    out_w,
    *outs,
):
    *first, gate_keep, left, right, keep, send = outs
    if first:
        column_parts(gated_t[...], cotangent, first[0], out_slots, "dp")
    row_parts(normed_t, gate_low[...], gate_keep, gate_slots, "dp")
    split = left.shape[2]
    row_parts(normed_t, value_low[:, :split], left, value_slots[0], "dp")
    row_parts(normed_t, value_low[:, split:], right, value_slots[1], "dp")
    me = lax.axis_index("tensor")
    half, height, _ = keep.shape
    for place, slot in enumerate(order):
        start = pl.multiple_of((me ^ slot) * height, height)
        part = dot(gated_t[:, pl.ds(start, height)], out_w[...], "tn")
        (keep if place < half else send)[place % half] = part


def join_kernel(count, *refs):
    *terms, out = refs
    split = terms[0].shape[2]
    for parts, lanes in ((terms[:count], slice(0, split)), (terms[count:], slice(split, None))):
        total = parts[0][0]
        for part in parts[1:]:
            total = total + part[0]
        out[:, lanes] = total


def mixer_back_kernel(
    order,
    head_count,
    dy,
    p,
    bc,
    v,
    s,
    srow,
    state,
    seg,
    params,
    dx_out,
    keep,
    send,
    step_low,
    heads_out,
    xd_scratch,
    dxd_scratch,
    dbc_t,
    rows_pad,
):
    _, inner = dy.shape
    state_size = bc.shape[1] // 2
    head_size = inner // head_count
    heads = params[8:16, :LANES]
    rate = -jnp.exp(heads[1:2, :])
    dt = softplus(v[...])
    spread = head_map(inner, head_size)
    skip_wide = dot_exact(heads, spread)[2:3]
    columns = seg_columns(seg)
    seg_row = seg[...]
    last = columns[STRETCH - 1 : STRETCH, :]
    even = iota((STRETCH, LANES), 1) < head_size
    lane = iota((STRETCH, LANES), 1)
    shape = (STRETCH, STRETCH)
    causal_t = iota(shape, 1) >= iota(shape, 0)
    scan = scan_matrix(STRETCH, True)
    dt_wide = dot_exact(dt, spread)
    pv = p[...]
    x = pv * sigmoid(pv)
    xd_scratch[...] = x * dt_wide

    first, second = slice(0, STRETCH), slice(STRETCH, 2 * STRETCH)
    queries = bc[second, state_size:].astype(bf16)
    keys = bc[first, :state_size].astype(bf16)
    state_low = state[...].astype(bf16)
    factor = jnp.where(columns[second] == last, jnp.exp(s[second, :]), 0.0)
    dcarry = dy[second, :] * dot_exact(factor, spread)
    dcarry_low = dcarry.astype(bf16)
    dbc_t[state_size:, second] = dot(state_low, dcarry_low, "nt")
    dstate = dot(queries, dcarry_low, "tn").astype(bf16)
    ds_second = dot_exact(dcarry * dot(queries, state_low), spread, "nt")
    tail = jnp.where(
        columns[first] == last, jnp.exp(s[STRETCH - 1 : STRETCH, :] - s[first, :]), 0.0
    )
    tail_wide = dot_exact(tail, spread)
    tailed = xd_scratch[first, :] * tail_wide
    dbc_t[:state_size, first] = dot(dstate, tailed.astype(bf16), "nt")
    dbc_t[state_size:, first] = jnp.zeros((state_size, STRETCH), f32)
    dbc_t[:state_size, second] = jnp.zeros((state_size, STRETCH), f32)
    dtailed = dot(keys, dstate)
    dxd_scratch[first, :] = dtailed * tail_wide
    dxd_scratch[second, :] = jnp.zeros((STRETCH, inner), f32)
    ds_tail = dot_exact(dtailed * tailed, spread, "nt")
    at = iota((STRETCH, LANES), 0)
    ds_first = jnp.where(at == STRETCH - 1, jnp.sum(ds_tail, axis=0, keepdims=True), 0.0) - ds_tail

    dskip = jnp.zeros((1, LANES), f32)
    ddecay = jnp.zeros((1, LANES), f32)
    dbias = jnp.zeros((1, LANES), f32)
    rows_pad[...] = jnp.zeros_like(rows_pad)
    for rows, ds in ((first, ds_first), (second, ds_second)):
        keys = bc[rows, :state_size].astype(bf16)
        queries = bc[rows, state_size:].astype(bf16)
        same = (columns[rows, 0:1] == seg_row[:, rows]) & causal_t
        scores = jnp.where(same, dot(keys, queries, "nt"), 0.0)
        dscores = jnp.zeros(shape, f32)
        for pair in range(inner // LANES):
            lanes = slice(pair * LANES, (pair + 1) * LANES)
            xd = xd_scratch[rows, lanes].astype(bf16)
            dyv = dy[rows, lanes].astype(bf16)
            found = []
            for place, head in enumerate((2 * pair, 2 * pair + 1)):
                gap = srow[head : head + 1, rows] - s[rows, head : head + 1]
                decay = jnp.exp(jnp.minimum(gap, 0.0))
                mine = even if place == 0 else jnp.logical_not(even)
                cross = dot(jnp.where(mine, xd, jnp.zeros_like(xd)), dyv, "nt")
                weight = decay * scores
                dscores = dscores + decay * cross
                moved = weight * cross
                ds = ds - jnp.where(lane == head, jnp.sum(moved, axis=1, keepdims=True), 0.0)
                rows_pad[head : head + 1, :] = jnp.sum(moved, axis=0, keepdims=True)
                found.append(dot(weight.astype(bf16), dyv))
            dxd_scratch[rows, lanes] += jnp.where(even, found[0], found[1])
        dscores = jnp.where(same, dscores, 0.0).astype(bf16)
        dbc_t[:state_size, rows] += dot(jnp.transpose(queries), dscores, "nt")
        dbc_t[state_size:, rows] += dot(jnp.transpose(keys), dscores)
        ds = ds + jnp.transpose(rows_pad[...])
        da = lax.dot_general(
            scan, ds, (((1,), (0,)), ((), ())), precision=highest, preferred_element_type=f32
        )
        pv = p[rows, :]
        x = pv * sigmoid(pv)
        dxd = dxd_scratch[rows, :]
        dyv = dy[rows, :]
        ddt = dot_exact(dxd * x, spread, "nt") + da * rate
        dx_out[rows, :] = dxd * dt_wide[rows] + dyv * skip_wide
        dstep = ddt * sigmoid(v[rows, :])
        step_low[rows, :] = dstep.astype(bf16)
        dbias = dbias + jnp.sum(dstep, axis=0, keepdims=True)
        ddecay = ddecay + jnp.sum(da * dt[rows], axis=0, keepdims=True)
        dskip = dskip + dot_exact(jnp.sum(dyv * x, axis=0, keepdims=True) + jnp.zeros((8, 1), f32), spread, "nt")[0:1]
    heads_out[...] = jnp.zeros_like(heads_out)
    heads_out[0:1, :] = dbias
    heads_out[1:2, :] = ddecay * rate
    heads_out[2:3, :] = dskip
    me = lax.axis_index("tensor")
    half, height, _ = keep.shape
    for place, slot in enumerate(order):
        start = pl.multiple_of((me ^ slot) * height, height)
        (keep if place < half else send)[place % half] = dbc_t[pl.ds(start, height), :]


def value_kernel(slots, dx, p, u, seg, params, normed_t, left, right, value_low, small):
    kernel_width = params.shape[0] - 20
    value_conv = params[:kernel_width]
    masks = delay_masks(seg_columns(seg), kernel_width)
    row_count, inner = dx.shape
    small[...] = jnp.zeros_like(small)
    for start in range(0, inner, LANES):
        lanes = slice(start, start + LANES)
        pv, uv = p[:, lanes], u[:, lanes]
        sig = sigmoid(pv)
        gp = dx[:, lanes] * (sig * (1.0 + pv * (1.0 - sig)))
        du = value_conv[kernel_width - 1 :, lanes] * gp
        small[kernel_width - 1 : kernel_width, lanes] = jnp.sum(gp * uv, axis=0, keepdims=True)
        small[kernel_width : kernel_width + 1, lanes] = jnp.sum(gp, axis=0, keepdims=True)
        for delay, mask in masks.items():
            tap = kernel_width - 1 - delay
            masked = gp * mask
            du = du + value_conv[tap : tap + 1, lanes] * pltpu.roll(masked, row_count - delay, 0)
            small[tap : tap + 1, lanes] = jnp.sum(
                masked * pltpu.roll(uv, delay, 0), axis=0, keepdims=True
            )
        value_low[:, lanes] = du.astype(bf16)
    split = left.shape[2]
    row_parts(normed_t, value_low[:, :split], left, slots[0], "dp")
    row_parts(normed_t, value_low[:, split:], right, slots[1], "dp")


def normed_kernel(
    dp_order,
    order,
    states_keep,
    states_got,
    states_last,
    normed_t,
    state_w,
    params,
    seg,
    gate_low,
    value_low,
    step_low,
    gate_w,
    value_w,
    step_w_t,
    tokens,
    small,
    gain_row,
    heads,
    keep,
    send,
    nk_keep,
    nk_send,
    step_pad,
    raw_t,
    conv_pad,
    conv_t,
    low_full,
    narrow_full,
    total,
    packed,
):
    kernel_width = params.shape[0] - 20
    state_width = state_w.shape[1]
    head_count = step_w_t.shape[0]
    _, own, row_count = states_keep.shape
    model_width = state_w.shape[0]
    rank = lax.axis_index("tensor")
    own_rows = pl.ds(pl.multiple_of(rank * own, own), own)
    step_pad[...] = jnp.zeros_like(step_pad)
    step_pad[:head_count, :] = step_w_t[...]
    raw_t[...] = dot(state_w[...], normed_t[...], "tn")
    conv_pad[...] = jnp.zeros_like(conv_pad)
    conv_pad[: kernel_width + 1, :] = params[16 : 17 + kernel_width, :state_width]
    conv_t[...] = jnp.transpose(conv_pad[...])
    raw = raw_t[own_rows, :]
    conv = conv_t[own_rows, :]
    seg_row = jnp.broadcast_to(seg[...], (8, row_count))
    at = iota((8, row_count), 1)
    p = conv[:, kernel_width : kernel_width + 1] + conv[:, kernel_width - 1 : kernel_width] * raw
    masks = {}
    for delay in range(1, kernel_width):
        tap = kernel_width - 1 - delay
        mask = jnp.where((pltpu.roll(seg_row, delay, 1) == seg_row) & (at >= delay), 1.0, 0.0)
        masks[delay] = mask[0:1]
        p = p + conv[:, tap : tap + 1] * (pltpu.roll(raw, delay, 1) * masks[delay])
    sig = sigmoid(p)
    gp = (states_keep[0] + states_got[0] + states_last[0]) * (sig * (1.0 + p * (1.0 - sig)))
    du = conv[:, kernel_width - 1 : kernel_width] * gp
    lane = iota((own, LANES), 1)

    def put(column, value):
        return jnp.where(lane == column, jnp.sum(value, axis=1, keepdims=True), 0.0)

    grads = put(kernel_width - 1, gp * raw) + put(kernel_width, gp)
    for delay, mask in masks.items():
        tap = kernel_width - 1 - delay
        masked = gp * mask
        du = du + conv[:, tap : tap + 1] * pltpu.roll(masked, row_count - delay, 1)
        grads = grads + put(tap, masked * pltpu.roll(raw, delay, 1))
    state_low = du.astype(bf16)
    narrow_full[:own, :] = dot(state_low, normed_t[...], "nt")
    step_rows = jnp.transpose(step_low[...].astype(f32))[:head_count].astype(bf16)
    narrow_full[own:, :] = dot(step_rows, normed_t[...], "nt")
    low_full[...] = jnp.zeros_like(low_full)
    low_full[own_rows, :] = state_low
    total[...] = dot(gate_low[...], gate_w[...], "nt")
    total[...] += dot(value_low[...], value_w[...], "nt")
    total[...] += dot(step_low[...], step_pad[...])
    total[...] += dot(
        jnp.transpose(low_full[...].astype(f32)).astype(bf16), state_w[...], "nt"
    )
    part = jnp.zeros((1, model_width), f32)
    for start in range(0, row_count, LANES):
        rows = slice(start, start + LANES)
        values = tokens[rows, :].astype(f32)
        inv = lax.rsqrt(jnp.mean(values * values, axis=-1, keepdims=True) + epsilon)
        part = part + jnp.sum(total[rows, :] * (values * inv), axis=0, keepdims=True)
    inner = packed.shape[1]
    packed[...] = jnp.zeros_like(packed)
    packed[: kernel_width + 1, :] = small[: kernel_width + 1, :]
    base = kernel_width + 1
    packed[base : base + 1, :] = gain_row[...]
    for start in range(0, model_width, inner):
        base += 1
        packed[base : base + 1, :] = part[:, start : start + inner]
    base += 1
    packed[base : base + 3, :LANES] = heads[0:3, :]
    base += 3
    packed[base : base + kernel_width + 1, :own] = jnp.transpose(grads)[: kernel_width + 1]
    height = own + head_count
    if dp_order is None:
        nk_keep[...] = narrow_full[...]
        at_row = 0
    else:
        me = lax.axis_index("dp")
        half = len(dp_order) // 2
        for place, slot in enumerate(dp_order):
            start = pl.multiple_of((me ^ slot) * LANES, LANES)
            rows = pl.ds(place % half * height, height)
            (nk_keep if place < half else nk_send)[rows, :] = narrow_full[:, pl.ds(start, LANES)]
        at_row = half * height
    for start in range(0, inner, LANES):
        nk_send[at_row : at_row + 16, :] = packed[:, start : start + LANES]
        at_row += 16
    half, height, _ = keep.shape
    for place, slot in enumerate(order):
        start = pl.multiple_of((rank ^ slot) * height, height)
        (keep if place < half else send)[place % half] = total[pl.ds(start, height), :]


def small_step_kernel(keep, sent, got, keep_out, send_out):
    count, half = keep.shape[0], keep_out.shape[0]
    keep_out[...] = keep[:half, :] + got[:half, :]
    send_out[:half, :] = keep[half:, :] + got[half:count, :]
    send_out[half:, :] = sent[count:, :] + got[count:, :]


def small_layout(kernel_width, inner, model_width):
    gain = kernel_width + 1
    norm = gain + 1
    heads = norm + model_width // inner
    return gain, norm, heads


def small_last_kernel(layout, own, inner, keep, sent, got, narrow, sums, share):
    count = keep.shape[0]
    narrow[...] = keep[...] + got[:count, :]
    sums[...] = sent[count:, :] + got[count:, :]
    share[:own, :] = narrow[:own, :]
    share[own : own + 16, :] = sums[:16, :]
    _, norm, heads = layout
    at = own + 16
    for row in range(norm, heads):
        for group in range(inner // LANES):
            share[at : at + 1, :] = sums[16 * group + row : 16 * group + row + 1, :]
            at += 1


def finish_kernel(layout, own, parts, *refs):
    shares, (narrow, sums), refs = refs[:parts], refs[parts : parts + 2], refs[parts + 2 :]
    *outs, states, convs = refs
    norm_o, vconv_o, vbias_o, sconv_o, sbias_o, sb_o, dl_o, sk_o, gain_o, step_o, state_o = outs
    gain, _, heads = layout
    kernel_width, inner = vconv_o.shape
    rank = lax.axis_index("tensor")
    for slot, share in enumerate(shares):
        rows = pl.ds(pl.multiple_of((rank ^ slot) * own, own), own)
        states[rows, :] = share[:own, :]
        block = jnp.concatenate([share[own : own + 16, :], jnp.zeros((LANES - 16, LANES), f32)])
        convs[rows, :] = jnp.transpose(block)[:own]
    state_o[...] = jnp.transpose(states[...])
    turned = jnp.transpose(convs[...])[heads + 3 :]
    sconv_o[...] = turned[:kernel_width]
    sbias_o[...] = turned[kernel_width : kernel_width + 1]
    step_o[...] = narrow[own:, :]
    total = shares[0][own + 16 :, :]
    for share in shares[1:]:
        total = total + share[own + 16 :, :]
    for place in range(total.shape[0]):
        norm_o[:, place * LANES : (place + 1) * LANES] = total[place : place + 1]
    for group in range(inner // LANES):
        lanes = slice(group * LANES, (group + 1) * LANES)
        block = sums[16 * group : 16 * group + 16, :]
        vconv_o[:, lanes] = block[:kernel_width]
        vbias_o[:, lanes] = block[kernel_width : kernel_width + 1]
        gain_o[:, lanes] = block[gain : gain + 1]
        if group == 0:
            for place, out in enumerate((sb_o, dl_o, sk_o)):
                out[...] = block[heads + place : heads + place + 1, : out.shape[1]]


def own_share(whole, scratch, sem):
    height = scratch.shape[0]
    start = pl.multiple_of(lax.axis_index("tensor") * height, height)
    return pltpu.make_async_copy(whole.at[pl.ds(start, height), :], scratch, sem)


def tokens_kernel(keep, got, last, norm_gain, tokens, cotangent, out, mine, theirs, sems):
    first, second = own_share(tokens, mine, sems.at[0]), own_share(cotangent, theirs, sems.at[1])
    first.start()
    second.start()
    first.wait()
    second.wait()
    model_width = tokens.shape[1]
    grad = keep[0] + got[0] + last[0]
    values = mine[...].astype(f32)
    inv = lax.rsqrt(jnp.mean(values * values, axis=-1, keepdims=True) + epsilon)
    scaled = grad * norm_gain[...]
    sums = jnp.sum(scaled * values, axis=-1, keepdims=True)
    out[...] = (
        scaled * inv
        - values * (inv * inv * inv) * sums / model_width
        + theirs[...].astype(f32)
    ).astype(bf16)


def mixed_kernel(keep, got, last, tokens, out, mine, sem):
    copy = own_share(tokens, mine, sem)
    copy.start()
    copy.wait()
    out[...] = (mine[...].astype(f32) + (keep[0] + got[0] + last[0])).astype(bf16)


def call(kernel, outs, args, scratch=(), cost=None, whole=0):
    vmem = pl.BlockSpec(memory_space=pltpu.VMEM)
    return pl.pallas_call(
        kernel,
        out_shape=[jax.ShapeDtypeStruct(shape, kind) for shape, kind in outs],
        in_specs=[vmem] * (len(args) - whole) + [pl.BlockSpec(memory_space=pltpu.HBM)] * whole,
        out_specs=[vmem] * len(outs),
        scratch_shapes=[
            piece if callable(getattr(piece, "get_array_aval", None)) else pltpu.VMEM(*piece)
            for piece in scratch
        ],
        compiler_params=pltpu.CompilerParams(vmem_limit_bytes=VMEM_LIMIT),
        cost_estimate=cost,
    )(*args)


def cost(flops, moved):
    return pl.CostEstimate(flops=int(flops), bytes_accessed=int(moved), transcendentals=0)


def body(
    tokens,
    cotangent,
    segment,
    norm_gain,
    gate_weight,
    value_weight,
    step_weight,
    state_weight,
    value_conv,
    value_conv_bias,
    state_conv,
    state_conv_bias,
    step_bias,
    decay_log,
    skip_gain,
    gated_gain,
    out_weight,
):
    row_count, model_width = tokens.shape
    tensor_parts = lax.axis_size("tensor")
    dp_parts = lax.axis_size("dp")
    share = row_count // tensor_parts
    heads_here = step_weight.shape[1]
    inner = gate_weight.shape[1]
    inner_total = inner * tensor_parts
    state_width = state_weight.shape[1]
    state_size = state_width // 2
    own_states = state_width // tensor_parts
    kernel_width = value_conv.shape[0]
    tensor_bits, dp_bits = bits_of(tensor_parts), bits_of(dp_parts)
    tensor_order = slot_order(tensor_bits)
    bits = {name: arranged(dp_bits, way) for name, way in WAYS.items()}
    order = {name: slot_order(way) for name, way in bits.items()}
    shard = model_width // dp_parts
    aligned = shard % LANES == 0
    assert row_count == SEQ_LEN == 2 * STRETCH and inner // heads_here * 2 == LANES

    def row(array):
        return array.reshape(1, -1)

    step_t = step_weight.T
    gain_rows = model_width // inner
    assert kernel_width + 2 + gain_rows <= 8 and row_count <= inner

    def at_rows(array, start):
        rows, width = array.shape
        return jnp.pad(array.astype(f32), ((start, 20 + kernel_width - start - rows), (0, inner - width)))

    params = (
        at_rows(value_conv, 0)
        + at_rows(row(value_conv_bias), kernel_width)
        + at_rows(row(gated_gain), kernel_width + 1)
        + at_rows(norm_gain.reshape(gain_rows, inner), kernel_width + 2)
        + at_rows(row(step_bias), 8)
        + at_rows(row(decay_log), 9)
        + at_rows(row(skip_gain), 10)
        + at_rows(state_conv, 16)
        + at_rows(row(state_conv_bias), 16 + kernel_width)
        + at_rows(row(segment), 17 + kernel_width)
    )
    normed, normed_t, seg = call(
        norm_kernel,
        [
            ((row_count, model_width), bf16),
            ((model_width, row_count), bf16),
            ((1, row_count), f32),
        ],
        [params, tokens],
        cost=cost(1e6, 3e6),
    )
    y, u, p, bc, v, s, srow, state = call(
        forward_kernel,
        [
            ((row_count, inner), f32),
            ((row_count, inner), f32),
            ((row_count, inner), f32),
            ((row_count, state_width), f32),
            ((row_count, LANES), f32),
            ((row_count, LANES), f32),
            ((heads_here, row_count), f32),
            ((state_size, inner), f32),
        ],
        [
            normed,
            seg,
            value_weight,
            step_t,
            state_weight,
            params,
        ],
        [((LANES, model_width), bf16), ((row_count, inner), f32)],
        cost=cost(3e9, 10e6),
    )
    z, gg, rows = call(
        gate_forward_kernel,
        [((row_count, inner), f32), ((row_count, inner), f32), ((8, row_count), f32)],
        [normed, y, gate_weight, cotangent, out_weight, params],
        cost=cost(2e9, 6e6),
    )
    for bit in tensor_bits[:-1]:
        rows = rows + swap(rows, "tensor", bit)
    rows_got = swap(rows, "tensor", tensor_bits[-1])

    half = dp_parts // 2
    (scaled_t,) = call(
        scaled_kernel, [((inner, row_count), f32)], [y, z, params], cost=cost(1e6, 3e6)
    )
    out_shape = ((half, inner, shard), f32) if aligned else ((inner, model_width), f32)
    out_send, gated_t = call(
        partial(out_send_kernel, inner_total, order["o"][half:] if aligned else None),
        [out_shape, ((inner, row_count), bf16)],
        [rows, rows_got, scaled_t, cotangent],
        cost=cost(1e9, 6e6),
    )
    gate_send, gate_low, dy, gain_row = call(
        partial(gate_send_kernel, inner_total, order["g"][half:]),
        [
            ((half, shard, inner), f32),
            ((row_count, inner), bf16),
            ((row_count, inner), f32),
            ((1, inner), f32),
        ],
        [rows, rows_got, y, z, gg, params, normed_t],
        [((LANES, row_count), f32)],
        cost=cost(1e9, 7e6),
    )
    row_shares = [((tensor_parts // 2, share, model_width), f32)] * 2
    dx, states_keep, states_send, step_low, head_sums = call(
        partial(mixer_back_kernel, tensor_order, heads_here),
        [
            ((row_count, inner), f32),
            ((tensor_parts // 2, own_states, row_count), f32),
            ((tensor_parts // 2, own_states, row_count), f32),
            ((row_count, LANES), bf16),
            ((8, LANES), f32),
        ],
        [dy, p, bc, v, s, srow, state, seg, params],
        [
            ((row_count, inner), f32),
            ((row_count, inner), f32),
            ((state_width, row_count), f32),
            ((LANES, STRETCH), f32),
        ],
        cost=cost(6e9, 8e6),
    )
    states = halving_parts(states_keep, states_send, "tensor", tensor_bits)
    split = inner // 2
    value_shapes = [((half, shard, split), f32), ((half, shard, inner - split), f32)]
    left_send, right_send, value_low, small = call(
        partial(value_kernel, (order["va"][half:], order["vb"][half:])),
        value_shapes + [((row_count, inner), bf16), ((8, inner), f32)],
        [dx, p, u, seg, params, normed_t],
        cost=cost(2e9, 7e6),
    )
    *out_keep, gate_keep, left_keep, right_keep, branch_keep, branch_send = call(
        partial(
            keep_kernel,
            order["o"][:half],
            order["g"][:half],
            (order["va"][:half], order["vb"][:half]),
            tensor_order,
        ),
        [out_shape] * aligned + [((half, shard, inner), f32)] + value_shapes + row_shares,
        [gated_t, cotangent, normed_t, gate_low, value_low, out_weight],
        cost=cost(3e9, 8e6),
    )
    if aligned:
        grad_out_shard = halving(out_keep[0], out_send, "dp", bits["o"])
    else:
        blocks = out_send.reshape(inner, dp_parts, shard)
        grad_out_shard = scatter_sum(jnp.swapaxes(blocks, 0, 1), "dp", dp_bits)
    gate_shard = halving(gate_keep, gate_send, "dp", bits["g"])
    left = halving_parts(left_keep, left_send, "dp", bits["va"])
    right = halving_parts(right_keep, right_send, "dp", bits["vb"])
    (value_shard,) = call(
        partial(join_kernel, len(left)), [((shard, inner), f32)], left + right, cost=cost(1e6, 2e6)
    )
    narrow_rows = own_states + heads_here
    group_rows = 16 * (inner // LANES)
    if aligned:
        small_shapes = [
            ((half * narrow_rows, LANES), f32),
            ((half * narrow_rows + group_rows, LANES), f32),
        ]
    else:
        small_shapes = [
            ((narrow_rows, model_width), f32),
            ((group_rows, LANES), f32),
        ]
    normed_keep, normed_send, small_keep, small_send = call(
        partial(normed_kernel, order["k"] if aligned else None, tensor_order),
        row_shares + small_shapes,
        [
            *states,
            normed_t,
            state_weight,
            params,
            seg,
            gate_low,
            value_low,
            step_low,
            gate_weight,
            value_weight,
            step_t,
            tokens,
            small,
            gain_row,
            head_sums,
        ],
        [
            ((LANES, model_width), bf16),
            ((state_width, row_count), f32),
            ((LANES, state_width), f32),
            ((state_width, LANES), f32),
            ((state_width, row_count), bf16),
            ((narrow_rows, model_width), f32),
            ((row_count, model_width), f32),
            ((16, inner), f32),
        ],
        cost=cost(4e9, 10e6),
    )
    normed_terms = halving_parts(normed_keep, normed_send, "tensor", tensor_bits)
    (grad_tokens,) = call(
        tokens_kernel,
        [((share, model_width), bf16)],
        [*normed_terms, row(norm_gain), tokens, cotangent],
        [((share, model_width), bf16)] * 2 + [pltpu.SemaphoreType.DMA((2,))],
        cost=cost(1e6, 2e6),
        whole=2,
    )
    branch_terms = halving_parts(branch_keep, branch_send, "tensor", tensor_bits)
    (mixed,) = call(
        mixed_kernel,
        [((share, model_width), bf16)],
        [*branch_terms, tokens],
        [((share, model_width), bf16), pltpu.SemaphoreType.DMA(())],
        cost=cost(1e6, 2e6),
        whole=1,
    )

    layout = small_layout(kernel_width, inner, model_width)
    sums_shape = ((group_rows, LANES), f32)
    share_rows = own_states + 16 + model_width // LANES
    last_shapes = [((narrow_rows, LANES), f32), sums_shape, ((share_rows, LANES), f32)]
    if aligned:
        count = half
        for bit in bits["k"]:
            small_got = swap(small_send, "dp", bit)
            if count > 1:
                count //= 2
                small_keep, small_send = call(
                    small_step_kernel,
                    [
                        ((count * narrow_rows, LANES), f32),
                        ((count * narrow_rows + sums_shape[0][0], LANES), f32),
                    ],
                    [small_keep, small_send, small_got],
                    cost=cost(1e6, 1e6),
                )
    else:
        split = small_keep.reshape(narrow_rows, dp_parts, shard)
        narrow = scatter_sum(jnp.swapaxes(split, 0, 1), "dp", dp_bits)
        small_keep = jnp.pad(narrow, ((0, 0), (0, LANES - shard)))
        sums = all_sum(small_send, "dp")
        small_send = jnp.concatenate([jnp.zeros_like(small_keep), sums])
        small_got = jnp.zeros_like(small_send)
    narrow, sums, shared = call(
        partial(small_last_kernel, layout, own_states, inner),
        last_shapes,
        [small_keep, small_send, small_got],
        cost=cost(1e6, 1e6),
    )
    shares = [shared]
    for slot in range(1, tensor_parts):
        shares.append(swap(shared, "tensor", slot))
    one = (1, inner)
    head_row = ((1, heads_here), f32)
    (
        norm_row,
        value_taps,
        value_bias,
        state_taps,
        state_bias,
        step_bias_row,
        decay_row,
        skip_row,
        gain_sum,
        step_grad,
        state_grad,
    ) = call(
        partial(finish_kernel, layout, own_states, tensor_parts),
        [
            ((1, model_width), f32),
            (value_conv.shape, f32),
            (one, f32),
            (state_conv.shape, f32),
            ((1, state_width), f32),
            head_row,
            head_row,
            head_row,
            (one, f32),
            ((heads_here, LANES), f32),
            ((LANES, state_width), f32),
        ],
        [*shares, narrow, sums],
        [((state_width, LANES), f32)] * 2,
        cost=cost(1e6, 1e6),
    )
    return (
        mixed,
        grad_tokens,
        norm_row.reshape(-1),
        gate_shard,
        value_shard,
        step_grad[:, :shard].T,
        state_grad[:shard],
        value_taps,
        value_bias.reshape(-1),
        state_taps,
        state_bias.reshape(-1),
        step_bias_row.reshape(-1),
        decay_row.reshape(-1),
        skip_row.reshape(-1),
        gain_sum.reshape(-1),
        grad_out_shard,
    )


def solution(mesh):
    return jax.shard_map(
        body,
        mesh=mesh,
        in_specs=(
            P("dp", None),
            P("dp", None),
            P("dp"),
            P(),
            P(None, "tensor"),
            P(None, "tensor"),
            P(None, "tensor"),
            P(),
            P(None, "tensor"),
            P("tensor"),
            P(),
            P(),
            P("tensor"),
            P("tensor"),
            P("tensor"),
            P("tensor"),
            P("tensor", None),
        ),
        out_specs=(
            P(("dp", "tensor"), None),
            P(("dp", "tensor"), None),
            P(),
            P("dp", "tensor"),
            P("dp", "tensor"),
            P("dp", "tensor"),
            P("dp", None),
            P(None, "tensor"),
            P("tensor"),
            P(),
            P(),
            P("tensor"),
            P("tensor"),
            P("tensor"),
            P("tensor"),
            P("tensor", "dp"),
        ),
        check_vma=False,
    )
```

```python
from functools import partial

import jax
import jax.numpy as jnp
from jax import lax
from jax.experimental import pallas as pl
from jax.experimental.pallas import tpu as pltpu
from jax.sharding import PartitionSpec as P


STRETCH = 256
SEQ_LEN = 512


epsilon = 1e-05
f32, bf16 = jnp.float32, jnp.bfloat16
LANES = 128
VMEM_LIMIT = 20 * 2**20
WAYS = {"o": "ynf", "g": "nyf", "va": "ynf", "vb": "ynf", "k": "nfy"}


def swap(array, axis, bit):
    size = lax.axis_size(axis)
    return lax.ppermute(array, axis, [(i, i ^ bit) for i in range(size)])


def bits_of(size):
    assert size & (size - 1) == 0
    return [1 << i for i in range(size.bit_length() - 1)]


def slot_order(bits):
    order = [0]
    for bit in reversed(bits):
        order = order + [slot | bit for slot in order]
    return order


def arranged(bits, way):
    parts = {"y": bits[:1], "n": bits[1:2], "f": bits[2:]}
    return [bit for name in way for bit in parts[name]]


def halving_parts(keep, send, axis, bits):
    terms, size = [keep], keep.shape[0]
    for bit in bits:
        terms.append(swap(send, axis, bit))
        half = size // 2
        if half:
            send = sum(term[half:size] for term in terms[1:]) + keep[half:size]
        size = half
    return terms


def halving(keep, send, axis, bits):
    terms = halving_parts(keep, send, axis, bits)
    first, *rest = [term[0] for term in terms]
    return first + sum(rest)


def scatter_sum(pieces, axis, bits):
    me = lax.axis_index(axis)
    slots = [lax.dynamic_index_in_dim(pieces, me ^ slot, 0) for slot in slot_order(bits)]
    half = len(slots) // 2
    return halving(jnp.concatenate(slots[:half]), jnp.concatenate(slots[half:]), axis, bits)


def all_sum(array, axis):
    for bit in bits_of(lax.axis_size(axis)):
        array = array + swap(array, axis, bit)
    return array


def dot(left, right, form="nn"):
    dims = {"nn": ((1,), (0,)), "nt": ((1,), (1,)), "tn": ((0,), (0,))}[form]
    return lax.dot_general(left, right, (dims, ((), ())), preferred_element_type=f32)


def dot_exact(left, right, form="nn"):
    high = left.astype(bf16)
    low = (left - high.astype(f32)).astype(bf16)
    return dot(high, right, form) + dot(low, right, form)


def scan_sum(ones, values):
    total, rest = None, values
    for _ in range(3):
        part = rest.astype(bf16)
        rest = rest - part.astype(f32)
        term = dot(ones, part)
        total = term if total is None else total + term
    return total


def widen(values, head_count, spread):
    high = values.astype(bf16).astype(f32)
    lane = iota(values.shape, 1)
    both = jnp.where(lane < head_count, high, pltpu.roll(values - high, head_count, 1))
    both = jnp.where(lane < 2 * head_count, both, 0.0)
    doubled = jnp.concatenate([spread[:head_count], spread[:head_count], spread[2 * head_count :]])
    return dot(both.astype(bf16), doubled)


def sigmoid(v):
    return 1.0 / (1.0 + jnp.exp(-v))


def softplus(v):
    return jnp.maximum(v, 0.0) + jnp.log1p(jnp.exp(-jnp.abs(v)))


def iota(shape, dim):
    return lax.broadcasted_iota(jnp.int32, shape, dim)


def head_map(width, head_size):
    shape = (LANES, width)
    return jnp.where(iota(shape, 0) == iota(shape, 1) // head_size, 1.0, 0.0).astype(bf16)


def seg_columns(seg_ref):
    row = seg_ref[...]
    return jnp.transpose(jnp.broadcast_to(row, (LANES, row.shape[1])))


def delay_masks(columns, kernel_width):
    at = iota(columns.shape, 0)
    return {
        delay: jnp.where((pltpu.roll(columns, delay, 0) == columns) & (at >= delay), 1.0, 0.0)
        for delay in range(1, kernel_width)
    }


def scan_matrix(size, upper):
    shape = (size, size)
    row, column = iota(shape, 0), iota(shape, 1)
    return jnp.where(column >= row if upper else column <= row, 1.0, 0.0).astype(bf16)


def conv_chunk(raw, masks, taps, bias):
    kernel_width = taps.shape[0]
    summed = bias + taps[kernel_width - 1 :] * raw
    for delay, mask in masks.items():
        tap = kernel_width - 1 - delay
        summed = summed + taps[tap : tap + 1] * (pltpu.roll(raw, delay, 0) * mask)
    return summed


def norm_kernel(tokens, norm_gain, normed, normed_t):
    gain = norm_gain[...]
    for start in range(0, tokens.shape[0], LANES):
        rows = slice(start, start + LANES)
        values = tokens[rows, :].astype(f32)
        inv = lax.rsqrt(jnp.mean(values * values, axis=-1, keepdims=True) + epsilon)
        values = values * inv * gain
        normed[rows, :] = values.astype(bf16)
        normed_t[:, rows] = jnp.transpose(values).astype(bf16)


def forward_kernel(
    normed,
    value_w,
    step_w_t,
    state_w,
    params,
    y_out,
    u_out,
    p_out,
    bc_out,
    v_out,
    s_out,
    srow_out,
    state_out,
    seg_out,
    step_pad,
    xd_scratch,
):
    row_count, inner = y_out.shape
    state_size = bc_out.shape[1] // 2
    head_count = step_w_t.shape[0]
    head_size = inner // head_count
    kernel_width = params.shape[0] - 20
    value_conv, value_bias = params[:kernel_width], params[kernel_width : kernel_width + 1]
    state_conv = params[16 : 16 + kernel_width, : 2 * state_size]
    state_bias = params[16 + kernel_width : 17 + kernel_width, : 2 * state_size]
    heads = params[8:16, :LANES]
    seg_out[...] = params[17 + kernel_width : 18 + kernel_width, :row_count]
    seg = seg_out
    step_pad[...] = jnp.zeros_like(step_pad)
    step_pad[:head_count, :] = step_w_t[...]
    v = dot(normed[...], step_pad[...], "nt") + heads[0:1, :]
    v_out[...] = v
    dt = softplus(v)
    rate = -jnp.exp(heads[1:2, :])
    spread = head_map(inner, head_size)
    scan = scan_matrix(STRETCH, False)
    for start in range(0, row_count, STRETCH):
        rows = slice(start, start + STRETCH)
        decay = scan_sum(scan, dt[rows] * rate)
        s_out[rows, :] = decay
        srow_out[:, rows] = jnp.transpose(decay)[: srow_out.shape[0]]
    columns = seg_columns(seg)
    masks = delay_masks(columns, kernel_width)
    bc_out[...] = dot(normed[...], state_w[...])
    for start in range(0, 2 * state_size, LANES):
        lanes = slice(start, start + LANES)
        p = conv_chunk(bc_out[:, lanes], masks, state_conv[:, lanes], state_bias[:, lanes])
        bc_out[:, lanes] = p * sigmoid(p)
    u_out[...] = dot(normed[...], value_w[...])
    dt_wide = widen(dt, head_count, spread)
    for start in range(0, inner, LANES):
        lanes = slice(start, start + LANES)
        p = conv_chunk(u_out[:, lanes], masks, value_conv[:, lanes], value_bias[:, lanes])
        p_out[:, lanes] = p
        x = p * sigmoid(p)
        xd_scratch[:, lanes] = x * dt_wide[:, lanes]
        skip = dot_exact(heads, spread[:, lanes])[2:3]
        y_out[:, lanes] = x * skip
    even = iota((STRETCH, LANES), 1) < head_size
    shape = (STRETCH, STRETCH)
    causal = iota(shape, 0) >= iota(shape, 1)
    seg_row = seg[...]
    for start in range(0, row_count, STRETCH):
        rows = slice(start, start + STRETCH)
        keys = bc_out[rows, :state_size].astype(bf16)
        queries = bc_out[rows, state_size:].astype(bf16)
        same = (columns[rows, 0:1] == seg_row[:, rows]) & causal
        scores = jnp.where(same, dot(queries, keys, "nt"), 0.0)
        for pair in range(inner // LANES):
            lanes = slice(pair * LANES, (pair + 1) * LANES)
            xd = xd_scratch[rows, lanes].astype(bf16)
            for first in range(0, STRETCH, LANES):
                some = slice(start + first, start + first + LANES)
                seen = first + LANES
                found = []
                for head in (2 * pair, 2 * pair + 1):
                    gap = s_out[some, head : head + 1] - srow_out[head : head + 1, start : start + seen]
                    weight = jnp.exp(jnp.minimum(gap, 0.0)) * scores[first : first + LANES, :seen]
                    found.append(dot(weight.astype(bf16), xd[:seen]))
                y_out[some, lanes] += jnp.where(even[:LANES], found[0], found[1])
        if start == 0:
            last = columns[STRETCH - 1 : STRETCH, :]
            tail = jnp.where(
                columns[rows] == last,
                jnp.exp(s_out[STRETCH - 1 : STRETCH, :] - s_out[rows, :]),
                0.0,
            )
            tailed = (xd_scratch[rows, :] * widen(tail, head_count, spread)).astype(bf16)
            state_out[...] = dot(keys, tailed, "tn")
        else:
            factor = jnp.where(columns[rows] == last, jnp.exp(s_out[rows, :]), 0.0)
            y_out[rows, :] += dot(queries, state_out[...].astype(bf16)) * widen(factor, head_count, spread)


def gate_forward_kernel(normed, y, gate_w, cotangent, out_w, params, z_out, gg_out, rows_out):
    row_count = y.shape[0]
    gated_gain = gain_of(params)
    z_out[...] = dot(normed[...], gate_w[...])
    gg_out[...] = dot(cotangent[...], out_w[...], "nt")
    z = z_out[...]
    gated_in = y[...] * (z * sigmoid(z))
    squares = jnp.sum(gated_in * gated_in, axis=-1, keepdims=True)
    dots = jnp.sum(gg_out[...] * gated_gain * gated_in, axis=-1, keepdims=True)
    lane = iota((row_count, LANES), 1)
    both = jnp.where(lane == 0, squares, jnp.where(lane == 1, dots, 0.0))
    rows_out[...] = jnp.transpose(both)[: rows_out.shape[0]]


def gain_of(params):
    row = params.shape[0] - 19
    return params[row : row + 1, :]


def scaled_kernel(y, z, params, scaled_t):
    zv = z[...]
    scaled_t[...] = jnp.transpose((y[...] * (zv * sigmoid(zv))) * gain_of(params))


def column_parts(matrix_t, columns, out, slots, axis):
    if slots is None:
        out[...] = dot(matrix_t, columns[...])
        return
    me = lax.axis_index(axis)
    width = out.shape[2]
    for place, slot in enumerate(slots):
        start = pl.multiple_of((me ^ slot) * width, width)
        out[place] = dot(matrix_t, columns[:, pl.ds(start, width)])


def row_parts(matrix_t, low, out, slots, axis):
    me = lax.axis_index(axis)
    height = out.shape[1]
    for place, slot in enumerate(slots):
        start = pl.multiple_of((me ^ slot) * height, height)
        out[place] = dot(matrix_t[pl.ds(start, height), :], low)


def out_send_kernel(inner_total, slots, rows, rows_got, scaled_t, cotangent, send, gated_t):
    inv = lax.rsqrt((rows[0:1, :] + rows_got[0:1, :]) / inner_total + epsilon)
    gated_t[...] = (scaled_t[...] * inv).astype(bf16)
    column_parts(gated_t[...], cotangent, send, slots, "dp")


def gate_send_kernel(
    inner_total,
    slots,
    rows,
    rows_got,
    y,
    z,
    gg,
    params,
    normed_t,
    send,
    gate_low,
    dy_out,
    gain_out,
    rows_pad,
):
    rows_pad[...] = jnp.zeros_like(rows_pad)
    rows_pad[: rows.shape[0], :] = rows[...] + rows_got[...]
    col = jnp.transpose(rows_pad[...])
    inv = lax.rsqrt(col[:, 0:1] / inner_total + epsilon)
    scale = inv * inv * inv * col[:, 1:2] / inner_total
    gated_gain = gain_of(params)
    for start in range(0, y.shape[1], LANES):
        lanes = slice(start, start + LANES)
        zv, yv, ggv = z[:, lanes], y[:, lanes], gg[:, lanes]
        sig = sigmoid(zv)
        silu = zv * sig
        gated_in = yv * silu
        mixer = ggv * gated_gain[:, lanes] * inv - gated_in * scale
        gain_out[:, lanes] = jnp.sum(ggv * gated_in * inv, axis=0, keepdims=True)
        dy_out[:, lanes] = mixer * silu
        gate_low[:, lanes] = (mixer * yv * (sig * (1.0 + zv * (1.0 - sig)))).astype(bf16)
    row_parts(normed_t, gate_low[...], send, slots, "dp")


def keep_kernel(
    out_slots,
    gate_slots,
    value_slots,
    order,
    gated_t,
    cotangent,
    normed_t,
    gate_low,
    value_low,
    out_w,
    *outs,
):
    *first, gate_keep, left, right, keep, send = outs
    if first:
        column_parts(gated_t[...], cotangent, first[0], out_slots, "dp")
    row_parts(normed_t, gate_low[...], gate_keep, gate_slots, "dp")
    split = left.shape[2]
    row_parts(normed_t, value_low[:, :split], left, value_slots[0], "dp")
    row_parts(normed_t, value_low[:, split:], right, value_slots[1], "dp")
    me = lax.axis_index("tensor")
    half, height, _ = keep.shape
    for place, slot in enumerate(order):
        start = pl.multiple_of((me ^ slot) * height, height)
        part = dot(gated_t[:, pl.ds(start, height)], out_w[...], "tn")
        (keep if place < half else send)[place % half] = part


def join_kernel(count, *refs):
    *terms, out = refs
    split = terms[0].shape[2]
    for parts, lanes in ((terms[:count], slice(0, split)), (terms[count:], slice(split, None))):
        total = parts[0][0]
        for part in parts[1:]:
            total = total + part[0]
        out[:, lanes] = total


def mixer_back_kernel(
    order,
    head_count,
    dy,
    p,
    bc,
    v,
    s,
    srow,
    state,
    seg,
    params,
    dx_out,
    keep,
    send,
    step_low,
    heads_out,
    xd_scratch,
    dxd_scratch,
    dbc_t,
    rows_pad,
):
    _, inner = dy.shape
    state_size = bc.shape[1] // 2
    head_size = inner // head_count
    heads = params[8:16, :LANES]
    rate = -jnp.exp(heads[1:2, :])
    dt = softplus(v[...])
    spread = head_map(inner, head_size)
    skip_wide = dot_exact(heads, spread)[2:3]
    columns = seg_columns(seg)
    seg_row = seg[...]
    last = columns[STRETCH - 1 : STRETCH, :]
    even = iota((STRETCH, LANES), 1) < head_size
    lane = iota((STRETCH, LANES), 1)
    shape = (STRETCH, STRETCH)
    causal_t = iota(shape, 1) >= iota(shape, 0)
    scan = scan_matrix(STRETCH, True)
    dt_wide = widen(dt, head_count, spread)
    pv = p[...]
    x = pv * sigmoid(pv)
    xd_scratch[...] = x * dt_wide

    first, second = slice(0, STRETCH), slice(STRETCH, 2 * STRETCH)
    queries = bc[second, state_size:].astype(bf16)
    keys = bc[first, :state_size].astype(bf16)
    state_low = state[...].astype(bf16)
    factor = jnp.where(columns[second] == last, jnp.exp(s[second, :]), 0.0)
    dcarry = dy[second, :] * widen(factor, head_count, spread)
    dcarry_low = dcarry.astype(bf16)
    dbc_t[state_size:, second] = dot(state_low, dcarry_low, "nt")
    dstate = dot(queries, dcarry_low, "tn").astype(bf16)
    ds_second = dot_exact(dcarry * dot(queries, state_low), spread, "nt")
    tail = jnp.where(
        columns[first] == last, jnp.exp(s[STRETCH - 1 : STRETCH, :] - s[first, :]), 0.0
    )
    tail_wide = widen(tail, head_count, spread)
    tailed = xd_scratch[first, :] * tail_wide
    dbc_t[:state_size, first] = dot(dstate, tailed.astype(bf16), "nt")
    dbc_t[state_size:, first] = jnp.zeros((state_size, STRETCH), f32)
    dbc_t[:state_size, second] = jnp.zeros((state_size, STRETCH), f32)
    dtailed = dot(keys, dstate)
    dxd_scratch[first, :] = dtailed * tail_wide
    dxd_scratch[second, :] = jnp.zeros((STRETCH, inner), f32)
    ds_tail = dot_exact(dtailed * tailed, spread, "nt")
    at = iota((STRETCH, LANES), 0)
    ds_first = jnp.where(at == STRETCH - 1, jnp.sum(ds_tail, axis=0, keepdims=True), 0.0) - ds_tail

    dskip = jnp.zeros((1, LANES), f32)
    ddecay = jnp.zeros((1, LANES), f32)
    dbias = jnp.zeros((1, LANES), f32)
    rows_pad[...] = jnp.zeros_like(rows_pad)
    for rows, ds in ((first, ds_first), (second, ds_second)):
        keys = bc[rows, :state_size].astype(bf16)
        queries = bc[rows, state_size:].astype(bf16)
        same = (columns[rows, 0:1] == seg_row[:, rows]) & causal_t
        scores = jnp.where(same, dot(keys, queries, "nt"), 0.0)
        dscores = jnp.zeros(shape, f32)
        for pair in range(inner // LANES):
            lanes = slice(pair * LANES, (pair + 1) * LANES)
            xd = xd_scratch[rows, lanes].astype(bf16)
            dyv = dy[rows, lanes].astype(bf16)
            found = []
            for place, head in enumerate((2 * pair, 2 * pair + 1)):
                gap = srow[head : head + 1, rows] - s[rows, head : head + 1]
                decay = jnp.exp(jnp.minimum(gap, 0.0))
                mine = even if place == 0 else jnp.logical_not(even)
                cross = dot(jnp.where(mine, xd, jnp.zeros_like(xd)), dyv, "nt")
                weight = decay * scores
                dscores = dscores + decay * cross
                moved = weight * cross
                ds = ds - jnp.where(lane == head, jnp.sum(moved, axis=1, keepdims=True), 0.0)
                rows_pad[head : head + 1, :] = jnp.sum(moved, axis=0, keepdims=True)
                found.append(dot(weight.astype(bf16), dyv))
            dxd_scratch[rows, lanes] += jnp.where(even, found[0], found[1])
        dscores = jnp.where(same, dscores, 0.0).astype(bf16)
        dbc_t[:state_size, rows] += dot(jnp.transpose(queries), dscores, "nt")
        dbc_t[state_size:, rows] += dot(jnp.transpose(keys), dscores)
        ds = ds + jnp.transpose(rows_pad[...])
        da = scan_sum(scan, ds)
        pv = p[rows, :]
        x = pv * sigmoid(pv)
        dxd = dxd_scratch[rows, :]
        dyv = dy[rows, :]
        ddt = dot_exact(dxd * x, spread, "nt") + da * rate
        dx_out[rows, :] = dxd * dt_wide[rows] + dyv * skip_wide
        dstep = ddt * sigmoid(v[rows, :])
        step_low[rows, :] = dstep.astype(bf16)
        dbias = dbias + jnp.sum(dstep, axis=0, keepdims=True)
        ddecay = ddecay + jnp.sum(da * dt[rows], axis=0, keepdims=True)
        dskip = dskip + dot_exact(jnp.sum(dyv * x, axis=0, keepdims=True) + jnp.zeros((8, 1), f32), spread, "nt")[0:1]
    heads_out[...] = jnp.zeros_like(heads_out)
    heads_out[0:1, :] = dbias
    heads_out[1:2, :] = ddecay * rate
    heads_out[2:3, :] = dskip
    me = lax.axis_index("tensor")
    half, height, _ = keep.shape
    for place, slot in enumerate(order):
        start = pl.multiple_of((me ^ slot) * height, height)
        (keep if place < half else send)[place % half] = dbc_t[pl.ds(start, height), :]


def value_kernel(slots, dx, p, u, seg, params, normed_t, left, right, value_low, small):
    kernel_width = params.shape[0] - 20
    value_conv = params[:kernel_width]
    masks = delay_masks(seg_columns(seg), kernel_width)
    row_count, inner = dx.shape
    small[...] = jnp.zeros_like(small)
    for start in range(0, inner, LANES):
        lanes = slice(start, start + LANES)
        pv, uv = p[:, lanes], u[:, lanes]
        sig = sigmoid(pv)
        gp = dx[:, lanes] * (sig * (1.0 + pv * (1.0 - sig)))
        du = value_conv[kernel_width - 1 :, lanes] * gp
        small[kernel_width - 1 : kernel_width, lanes] = jnp.sum(gp * uv, axis=0, keepdims=True)
        small[kernel_width : kernel_width + 1, lanes] = jnp.sum(gp, axis=0, keepdims=True)
        for delay, mask in masks.items():
            tap = kernel_width - 1 - delay
            masked = gp * mask
            du = du + value_conv[tap : tap + 1, lanes] * pltpu.roll(masked, row_count - delay, 0)
            small[tap : tap + 1, lanes] = jnp.sum(
                masked * pltpu.roll(uv, delay, 0), axis=0, keepdims=True
            )
        value_low[:, lanes] = du.astype(bf16)
    split = left.shape[2]
    row_parts(normed_t, value_low[:, :split], left, slots[0], "dp")
    row_parts(normed_t, value_low[:, split:], right, slots[1], "dp")


def normed_kernel(
    dp_order,
    order,
    states_keep,
    states_got,
    states_last,
    normed_t,
    state_w,
    params,
    seg,
    gate_low,
    value_low,
    step_low,
    gate_w,
    value_w,
    step_w_t,
    tokens,
    small,
    gain_row,
    heads,
    keep,
    send,
    nk_keep,
    nk_send,
    step_pad,
    raw_t,
    conv_pad,
    conv_t,
    low_full,
    narrow_full,
    total,
    packed,
):
    kernel_width = params.shape[0] - 20
    state_width = state_w.shape[1]
    head_count = step_w_t.shape[0]
    _, own, row_count = states_keep.shape
    model_width = state_w.shape[0]
    rank = lax.axis_index("tensor")
    own_rows = pl.ds(pl.multiple_of(rank * own, own), own)
    step_pad[...] = jnp.zeros_like(step_pad)
    step_pad[:head_count, :] = step_w_t[...]
    raw_t[...] = dot(state_w[...], normed_t[...], "tn")
    conv_pad[...] = jnp.zeros_like(conv_pad)
    conv_pad[: kernel_width + 1, :] = params[16 : 17 + kernel_width, :state_width]
    conv_t[...] = jnp.transpose(conv_pad[...])
    raw = raw_t[own_rows, :]
    conv = conv_t[own_rows, :]
    seg_row = jnp.broadcast_to(seg[...], (8, row_count))
    at = iota((8, row_count), 1)
    p = conv[:, kernel_width : kernel_width + 1] + conv[:, kernel_width - 1 : kernel_width] * raw
    masks = {}
    for delay in range(1, kernel_width):
        tap = kernel_width - 1 - delay
        mask = jnp.where((pltpu.roll(seg_row, delay, 1) == seg_row) & (at >= delay), 1.0, 0.0)
        masks[delay] = mask[0:1]
        p = p + conv[:, tap : tap + 1] * (pltpu.roll(raw, delay, 1) * masks[delay])
    sig = sigmoid(p)
    gp = (states_keep[0] + states_got[0] + states_last[0]) * (sig * (1.0 + p * (1.0 - sig)))
    du = conv[:, kernel_width - 1 : kernel_width] * gp
    lane = iota((own, LANES), 1)

    def put(column, value):
        return jnp.where(lane == column, jnp.sum(value, axis=1, keepdims=True), 0.0)

    grads = put(kernel_width - 1, gp * raw) + put(kernel_width, gp)
    for delay, mask in masks.items():
        tap = kernel_width - 1 - delay
        masked = gp * mask
        du = du + conv[:, tap : tap + 1] * pltpu.roll(masked, row_count - delay, 1)
        grads = grads + put(tap, masked * pltpu.roll(raw, delay, 1))
    state_low = du.astype(bf16)
    narrow_full[:own, :] = dot(state_low, normed_t[...], "nt")
    step_rows = jnp.transpose(step_low[...].astype(f32))[:head_count].astype(bf16)
    narrow_full[own:, :] = dot(step_rows, normed_t[...], "nt")
    low_full[...] = jnp.zeros_like(low_full)
    low_full[own_rows, :] = state_low
    total[...] = dot(gate_low[...], gate_w[...], "nt")
    total[...] += dot(value_low[...], value_w[...], "nt")
    total[...] += dot(step_low[...], step_pad[...])
    total[...] += dot(
        jnp.transpose(low_full[...].astype(f32)).astype(bf16), state_w[...], "nt"
    )
    part = jnp.zeros((1, model_width), f32)
    for start in range(0, row_count, LANES):
        rows = slice(start, start + LANES)
        values = tokens[rows, :].astype(f32)
        inv = lax.rsqrt(jnp.mean(values * values, axis=-1, keepdims=True) + epsilon)
        part = part + jnp.sum(total[rows, :] * (values * inv), axis=0, keepdims=True)
    inner = packed.shape[1]
    packed[...] = jnp.zeros_like(packed)
    packed[: kernel_width + 1, :] = small[: kernel_width + 1, :]
    base = kernel_width + 1
    packed[base : base + 1, :] = gain_row[...]
    for start in range(0, model_width, inner):
        base += 1
        packed[base : base + 1, :] = part[:, start : start + inner]
    base += 1
    packed[base : base + 3, :LANES] = heads[0:3, :]
    base += 3
    packed[base : base + kernel_width + 1, :own] = jnp.transpose(grads)[: kernel_width + 1]
    height = own + head_count
    if dp_order is None:
        nk_keep[...] = narrow_full[...]
        at_row = 0
    else:
        me = lax.axis_index("dp")
        half = len(dp_order) // 2
        for place, slot in enumerate(dp_order):
            start = pl.multiple_of((me ^ slot) * LANES, LANES)
            rows = pl.ds(place % half * height, height)
            (nk_keep if place < half else nk_send)[rows, :] = narrow_full[:, pl.ds(start, LANES)]
        at_row = half * height
    for start in range(0, inner, LANES):
        nk_send[at_row : at_row + 16, :] = packed[:, start : start + LANES]
        at_row += 16
    half, height, _ = keep.shape
    for place, slot in enumerate(order):
        start = pl.multiple_of((rank ^ slot) * height, height)
        (keep if place < half else send)[place % half] = total[pl.ds(start, height), :]


def small_step_kernel(keep, sent, got, keep_out, send_out):
    count, half = keep.shape[0], keep_out.shape[0]
    keep_out[...] = keep[:half, :] + got[:half, :]
    send_out[:half, :] = keep[half:, :] + got[half:count, :]
    send_out[half:, :] = sent[count:, :] + got[count:, :]


def small_layout(kernel_width, inner, model_width):
    gain = kernel_width + 1
    norm = gain + 1
    heads = norm + model_width // inner
    return gain, norm, heads


def small_last_kernel(layout, own, inner, keep, sent, got, narrow, sums, share):
    count = keep.shape[0]
    narrow[...] = keep[...] + got[:count, :]
    sums[...] = sent[count:, :] + got[count:, :]
    share[:own, :] = narrow[:own, :]
    share[own : own + 16, :] = sums[:16, :]
    _, norm, heads = layout
    at = own + 16
    for row in range(norm, heads):
        for group in range(inner // LANES):
            share[at : at + 1, :] = sums[16 * group + row : 16 * group + row + 1, :]
            at += 1


def finish_kernel(layout, own, parts, *refs):
    shares, (narrow, sums), refs = refs[:parts], refs[parts : parts + 2], refs[parts + 2 :]
    *outs, states, convs = refs
    norm_o, vconv_o, vbias_o, sconv_o, sbias_o, sb_o, dl_o, sk_o, gain_o, step_o, state_o = outs
    gain, _, heads = layout
    kernel_width, inner = vconv_o.shape
    rank = lax.axis_index("tensor")
    for slot, share in enumerate(shares):
        rows = pl.ds(pl.multiple_of((rank ^ slot) * own, own), own)
        states[rows, :] = share[:own, :]
        block = jnp.concatenate([share[own : own + 16, :], jnp.zeros((LANES - 16, LANES), f32)])
        convs[rows, :] = jnp.transpose(block)[:own]
    state_o[...] = jnp.transpose(states[...])
    turned = jnp.transpose(convs[...])[heads + 3 :]
    sconv_o[...] = turned[:kernel_width]
    sbias_o[...] = turned[kernel_width : kernel_width + 1]
    step_o[...] = narrow[own:, :]
    total = shares[0][own + 16 :, :]
    for share in shares[1:]:
        total = total + share[own + 16 :, :]
    for place in range(total.shape[0]):
        norm_o[:, place * LANES : (place + 1) * LANES] = total[place : place + 1]
    for group in range(inner // LANES):
        lanes = slice(group * LANES, (group + 1) * LANES)
        block = sums[16 * group : 16 * group + 16, :]
        vconv_o[:, lanes] = block[:kernel_width]
        vbias_o[:, lanes] = block[kernel_width : kernel_width + 1]
        gain_o[:, lanes] = block[gain : gain + 1]
        if group == 0:
            for place, out in enumerate((sb_o, dl_o, sk_o)):
                out[...] = block[heads + place : heads + place + 1, : out.shape[1]]


def own_share(whole, scratch, sem):
    height = scratch.shape[0]
    start = pl.multiple_of(lax.axis_index("tensor") * height, height)
    return pltpu.make_async_copy(whole.at[pl.ds(start, height), :], scratch, sem)


def tokens_kernel(keep, got, last, norm_gain, tokens, cotangent, out, mine, theirs, sems):
    first, second = own_share(tokens, mine, sems.at[0]), own_share(cotangent, theirs, sems.at[1])
    first.start()
    second.start()
    first.wait()
    second.wait()
    model_width = tokens.shape[1]
    grad = keep[0] + got[0] + last[0]
    values = mine[...].astype(f32)
    inv = lax.rsqrt(jnp.mean(values * values, axis=-1, keepdims=True) + epsilon)
    scaled = grad * norm_gain[...]
    sums = jnp.sum(scaled * values, axis=-1, keepdims=True)
    out[...] = (
        scaled * inv
        - values * (inv * inv * inv) * sums / model_width
        + theirs[...].astype(f32)
    ).astype(bf16)


def mixed_kernel(keep, got, last, tokens, out, mine, sem):
    copy = own_share(tokens, mine, sem)
    copy.start()
    copy.wait()
    out[...] = (mine[...].astype(f32) + (keep[0] + got[0] + last[0])).astype(bf16)


def call(kernel, outs, args, scratch=(), cost=None, whole=0):
    vmem = pl.BlockSpec(memory_space=pltpu.VMEM)
    return pl.pallas_call(
        kernel,
        out_shape=[jax.ShapeDtypeStruct(shape, kind) for shape, kind in outs],
        in_specs=[vmem] * (len(args) - whole) + [pl.BlockSpec(memory_space=pltpu.HBM)] * whole,
        out_specs=[vmem] * len(outs),
        scratch_shapes=[
            piece if callable(getattr(piece, "get_array_aval", None)) else pltpu.VMEM(*piece)
            for piece in scratch
        ],
        compiler_params=pltpu.CompilerParams(vmem_limit_bytes=VMEM_LIMIT),
        cost_estimate=cost,
    )(*args)


def cost(flops, moved):
    return pl.CostEstimate(flops=int(flops), bytes_accessed=int(moved), transcendentals=0)


def body(
    tokens,
    cotangent,
    segment,
    norm_gain,
    gate_weight,
    value_weight,
    step_weight,
    state_weight,
    value_conv,
    value_conv_bias,
    state_conv,
    state_conv_bias,
    step_bias,
    decay_log,
    skip_gain,
    gated_gain,
    out_weight,
):
    row_count, model_width = tokens.shape
    tensor_parts = lax.axis_size("tensor")
    dp_parts = lax.axis_size("dp")
    share = row_count // tensor_parts
    heads_here = step_weight.shape[1]
    inner = gate_weight.shape[1]
    inner_total = inner * tensor_parts
    state_width = state_weight.shape[1]
    state_size = state_width // 2
    own_states = state_width // tensor_parts
    kernel_width = value_conv.shape[0]
    tensor_bits, dp_bits = bits_of(tensor_parts), bits_of(dp_parts)
    tensor_order = slot_order(tensor_bits)
    bits = {name: arranged(dp_bits, way) for name, way in WAYS.items()}
    order = {name: slot_order(way) for name, way in bits.items()}
    shard = model_width // dp_parts
    aligned = shard % LANES == 0
    assert row_count == SEQ_LEN == 2 * STRETCH and inner // heads_here * 2 == LANES

    def row(array):
        return array.reshape(1, -1)

    step_t = step_weight.T
    assert kernel_width + 2 <= 8 and row_count <= inner

    def at_rows(array, start):
        rows, width = array.shape
        space = ((start, 20 + kernel_width - start - rows), (0, inner - width))
        return jnp.pad(array, space).astype(f32)

    params = (
        at_rows(value_conv, 0)
        + at_rows(row(value_conv_bias), kernel_width)
        + at_rows(row(gated_gain), kernel_width + 1)
        + at_rows(row(step_bias), 8)
        + at_rows(row(decay_log), 9)
        + at_rows(row(skip_gain), 10)
        + at_rows(state_conv, 16)
        + at_rows(row(state_conv_bias), 16 + kernel_width)
        + at_rows(row(segment), 17 + kernel_width)
    )
    normed, normed_t = call(
        norm_kernel,
        [((row_count, model_width), bf16), ((model_width, row_count), bf16)],
        [tokens, row(norm_gain)],
        cost=cost(1e6, 3e6),
    )
    y, u, p, bc, v, s, srow, state, seg = call(
        forward_kernel,
        [
            ((row_count, inner), f32),
            ((row_count, inner), f32),
            ((row_count, inner), f32),
            ((row_count, state_width), f32),
            ((row_count, LANES), f32),
            ((row_count, LANES), f32),
            ((heads_here, row_count), f32),
            ((state_size, inner), f32),
            ((1, row_count), f32),
        ],
        [
            normed,
            value_weight,
            step_t,
            state_weight,
            params,
        ],
        [((LANES, model_width), bf16), ((row_count, inner), f32)],
        cost=cost(3e9, 10e6),
    )
    z, gg, rows = call(
        gate_forward_kernel,
        [((row_count, inner), f32), ((row_count, inner), f32), ((8, row_count), f32)],
        [normed, y, gate_weight, cotangent, out_weight, params],
        cost=cost(2e9, 6e6),
    )
    for bit in tensor_bits[:-1]:
        rows = rows + swap(rows, "tensor", bit)
    rows_got = swap(rows, "tensor", tensor_bits[-1])

    half = dp_parts // 2
    (scaled_t,) = call(
        scaled_kernel, [((inner, row_count), f32)], [y, z, params], cost=cost(1e6, 3e6)
    )
    out_shape = ((half, inner, shard), f32) if aligned else ((inner, model_width), f32)
    out_send, gated_t = call(
        partial(out_send_kernel, inner_total, order["o"][half:] if aligned else None),
        [out_shape, ((inner, row_count), bf16)],
        [rows, rows_got, scaled_t, cotangent],
        cost=cost(1e9, 6e6),
    )
    gate_send, gate_low, dy, gain_row = call(
        partial(gate_send_kernel, inner_total, order["g"][half:]),
        [
            ((half, shard, inner), f32),
            ((row_count, inner), bf16),
            ((row_count, inner), f32),
            ((1, inner), f32),
        ],
        [rows, rows_got, y, z, gg, params, normed_t],
        [((LANES, row_count), f32)],
        cost=cost(1e9, 7e6),
    )
    row_shares = [((tensor_parts // 2, share, model_width), f32)] * 2
    dx, states_keep, states_send, step_low, head_sums = call(
        partial(mixer_back_kernel, tensor_order, heads_here),
        [
            ((row_count, inner), f32),
            ((tensor_parts // 2, own_states, row_count), f32),
            ((tensor_parts // 2, own_states, row_count), f32),
            ((row_count, LANES), bf16),
            ((8, LANES), f32),
        ],
        [dy, p, bc, v, s, srow, state, seg, params],
        [
            ((row_count, inner), f32),
            ((row_count, inner), f32),
            ((state_width, row_count), f32),
            ((LANES, STRETCH), f32),
        ],
        cost=cost(6e9, 8e6),
    )
    states = halving_parts(states_keep, states_send, "tensor", tensor_bits)
    split = inner // 2
    value_shapes = [((half, shard, split), f32), ((half, shard, inner - split), f32)]
    left_send, right_send, value_low, small = call(
        partial(value_kernel, (order["va"][half:], order["vb"][half:])),
        value_shapes + [((row_count, inner), bf16), ((8, inner), f32)],
        [dx, p, u, seg, params, normed_t],
        cost=cost(2e9, 7e6),
    )
    *out_keep, gate_keep, left_keep, right_keep, branch_keep, branch_send = call(
        partial(
            keep_kernel,
            order["o"][:half],
            order["g"][:half],
            (order["va"][:half], order["vb"][:half]),
            tensor_order,
        ),
        [out_shape] * aligned + [((half, shard, inner), f32)] + value_shapes + row_shares,
        [gated_t, cotangent, normed_t, gate_low, value_low, out_weight],
        cost=cost(3e9, 8e6),
    )
    if aligned:
        grad_out_shard = halving(out_keep[0], out_send, "dp", bits["o"])
    else:
        blocks = out_send.reshape(inner, dp_parts, shard)
        grad_out_shard = scatter_sum(jnp.swapaxes(blocks, 0, 1), "dp", dp_bits)
    gate_shard = halving(gate_keep, gate_send, "dp", bits["g"])
    left = halving_parts(left_keep, left_send, "dp", bits["va"])
    right = halving_parts(right_keep, right_send, "dp", bits["vb"])
    (value_shard,) = call(
        partial(join_kernel, len(left)), [((shard, inner), f32)], left + right, cost=cost(1e6, 2e6)
    )
    narrow_rows = own_states + heads_here
    group_rows = 16 * (inner // LANES)
    if aligned:
        small_shapes = [
            ((half * narrow_rows, LANES), f32),
            ((half * narrow_rows + group_rows, LANES), f32),
        ]
    else:
        small_shapes = [
            ((narrow_rows, model_width), f32),
            ((group_rows, LANES), f32),
        ]
    normed_keep, normed_send, small_keep, small_send = call(
        partial(normed_kernel, order["k"] if aligned else None, tensor_order),
        row_shares + small_shapes,
        [
            *states,
            normed_t,
            state_weight,
            params,
            seg,
            gate_low,
            value_low,
            step_low,
            gate_weight,
            value_weight,
            step_t,
            tokens,
            small,
            gain_row,
            head_sums,
        ],
        [
            ((LANES, model_width), bf16),
            ((state_width, row_count), f32),
            ((LANES, state_width), f32),
            ((state_width, LANES), f32),
            ((state_width, row_count), bf16),
            ((narrow_rows, model_width), f32),
            ((row_count, model_width), f32),
            ((16, inner), f32),
        ],
        cost=cost(4e9, 10e6),
    )
    normed_terms = halving_parts(normed_keep, normed_send, "tensor", tensor_bits)
    (grad_tokens,) = call(
        tokens_kernel,
        [((share, model_width), bf16)],
        [*normed_terms, row(norm_gain), tokens, cotangent],
        [((share, model_width), bf16)] * 2 + [pltpu.SemaphoreType.DMA((2,))],
        cost=cost(1e6, 2e6),
        whole=2,
    )
    branch_terms = halving_parts(branch_keep, branch_send, "tensor", tensor_bits)
    (mixed,) = call(
        mixed_kernel,
        [((share, model_width), bf16)],
        [*branch_terms, tokens],
        [((share, model_width), bf16), pltpu.SemaphoreType.DMA(())],
        cost=cost(1e6, 2e6),
        whole=1,
    )

    layout = small_layout(kernel_width, inner, model_width)
    sums_shape = ((group_rows, LANES), f32)
    share_rows = own_states + 16 + model_width // LANES
    last_shapes = [((narrow_rows, LANES), f32), sums_shape, ((share_rows, LANES), f32)]
    if aligned:
        count = half
        for bit in bits["k"]:
            small_got = swap(small_send, "dp", bit)
            if count > 1:
                count //= 2
                small_keep, small_send = call(
                    small_step_kernel,
                    [
                        ((count * narrow_rows, LANES), f32),
                        ((count * narrow_rows + sums_shape[0][0], LANES), f32),
                    ],
                    [small_keep, small_send, small_got],
                    cost=cost(1e6, 1e6),
                )
    else:
        split = small_keep.reshape(narrow_rows, dp_parts, shard)
        narrow = scatter_sum(jnp.swapaxes(split, 0, 1), "dp", dp_bits)
        small_keep = jnp.pad(narrow, ((0, 0), (0, LANES - shard)))
        sums = all_sum(small_send, "dp")
        small_send = jnp.concatenate([jnp.zeros_like(small_keep), sums])
        small_got = jnp.zeros_like(small_send)
    narrow, sums, shared = call(
        partial(small_last_kernel, layout, own_states, inner),
        last_shapes,
        [small_keep, small_send, small_got],
        cost=cost(1e6, 1e6),
    )
    shares = [shared]
    for slot in range(1, tensor_parts):
        shares.append(swap(shared, "tensor", slot))
    one = (1, inner)
    head_row = ((1, heads_here), f32)
    (
        norm_row,
        value_taps,
        value_bias,
        state_taps,
        state_bias,
        step_bias_row,
        decay_row,
        skip_row,
        gain_sum,
        step_grad,
        state_grad,
    ) = call(
        partial(finish_kernel, layout, own_states, tensor_parts),
        [
            ((1, model_width), f32),
            (value_conv.shape, f32),
            (one, f32),
            (state_conv.shape, f32),
            ((1, state_width), f32),
            head_row,
            head_row,
            head_row,
            (one, f32),
            ((heads_here, LANES), f32),
            ((LANES, state_width), f32),
        ],
        [*shares, narrow, sums],
        [((state_width, LANES), f32)] * 2,
        cost=cost(1e6, 1e6),
    )
    return (
        mixed,
        grad_tokens,
        norm_row.reshape(-1),
        gate_shard,
        value_shard,
        step_grad[:, :shard].T,
        state_grad[:shard],
        value_taps,
        value_bias.reshape(-1),
        state_taps,
        state_bias.reshape(-1),
        step_bias_row.reshape(-1),
        decay_row.reshape(-1),
        skip_row.reshape(-1),
        gain_sum.reshape(-1),
        grad_out_shard,
    )


def solution(mesh):
    return jax.shard_map(
        body,
        mesh=mesh,
        in_specs=(
            P("dp", None),
            P("dp", None),
            P("dp"),
            P(),
            P(None, "tensor"),
            P(None, "tensor"),
            P(None, "tensor"),
            P(),
            P(None, "tensor"),
            P("tensor"),
            P(),
            P(),
            P("tensor"),
            P("tensor"),
            P("tensor"),
            P("tensor"),
            P("tensor", None),
        ),
        out_specs=(
            P(("dp", "tensor"), None),
            P(("dp", "tensor"), None),
            P(),
            P("dp", "tensor"),
            P("dp", "tensor"),
            P("dp", "tensor"),
            P("dp", None),
            P(None, "tensor"),
            P("tensor"),
            P(),
            P(),
            P("tensor"),
            P("tensor"),
            P("tensor"),
            P("tensor"),
            P("tensor", "dp"),
        ),
        check_vma=False,
    )
```
